32 devices in a mesh: gx: 2 (over core), gy: 4 (over y, x), gz: 4 (over z).
Axes of the slice: x: 2, y: 2, z: 4, core: 2. Of those that a mesh axis runs over, the one named last changes fastest.
Arguments:
- basis: float32 [32, 262144], P(None, ('gx', 'gy', 'gz')), may hold values from -5.5 to 5.5
- sigma: float32 [32], replicated, may hold values from 1 to 8
- snapshots: float32 [64, 262144], P(None, ('gx', 'gy', 'gz')), may hold values from -200 to 200
Outputs:
- modes: float32 [32, 262144], P(None, ('gx', 'gy', 'gz'))
- values: float32 [32], replicated
The draws below stay inside these ranges and needn't reach their ends.
All inputs are finite; a program needn't handle non-finite values.
Results may differ from the reference program's by a relative error of at most 0.00016.
Values sent between devices are 32-bit elements; how exact they have to be, the bound alone decides.
No kernel may reach another device: no remote copies, remote signals or barrier semaphores. Data moves between devices by JAX's collectives and lax.ppermute only.
A program may use at most 64 MiB of HBM per device.

```python
import math
import jax
import jax.numpy as jnp
from jax import lax

K = 32
NEW = 64
ITERS = 4
ROWS = 262144


def common_basis(key):
    basis_key = jax.random.fold_in(key, 11)
    sample = jnp.clip(jax.random.normal(basis_key, (K, ROWS), jnp.float32), -5.0, 5.0)
    return sample + 0.05 * jnp.roll(sample, 1, axis=0)


def draw_basis(key, part):
    return common_basis(key)


def draw_snapshots(key, part):
    basis = common_basis(key)
    mixing = jax.random.normal(jax.random.fold_in(key, 12), (K, NEW), jnp.float32)
    noise_key = jax.random.fold_in(key, 13)
    spread_key = jax.random.fold_in(key, 14)
    noise = jax.random.normal(noise_key, (NEW, ROWS), jnp.float32)
    spread = jnp.exp(jax.random.uniform(spread_key, (ROWS,), jnp.float32, -0.3566749, 0.3364722))
    place = jnp.arange(ROWS, dtype=jnp.float32) / ROWS
    rising = 0.5 + place
    signal = jnp.dot(mixing.T, basis, precision=lax.Precision.HIGHEST) * rising
    return jnp.clip(signal + 0.5 * spread * noise, -200.0, 200.0)


def setup_inputs(seed: int = 0) -> dict:
    keys = jax.random.split(jax.random.key(seed), 4)
    return {
        "basis": draw_basis(jax.random.fold_in(keys[3], 71), 0),
        "sigma": jnp.clip(jnp.exp(jax.random.uniform(keys[1], (K,), jnp.float32, math.log(1.0), math.log(8.0))), 1.0, 8.0),
        "snapshots": draw_snapshots(jax.random.fold_in(keys[3], 71), 0),
    }


HIGH = lax.Precision.HIGHEST

def inner(left, right, total):
    product = lax.dot_general(left.astype(jnp.float32), right.astype(jnp.float32), (((1,), (1,)), ((), ())), precision=HIGH, preferred_element_type=jnp.float32)
    return product / total

def orthonormal(block):
    for repeat in range(2):
        factor = jnp.linalg.cholesky(jnp.dot(block.T, block, precision=HIGH))
        block = jax.scipy.linalg.solve_triangular(factor, block.T, lower=True).T
    return block

def rotate(sigma, coeffs, factor):
    modes_count = sigma.shape[0]
    fresh_count = factor.shape[0]
    upper_rows = jnp.concatenate([jnp.diag(sigma), coeffs], axis=1)
    lower_rows = jnp.concatenate([jnp.zeros((fresh_count, modes_count), jnp.float32), factor], axis=1)
    core = jnp.concatenate([upper_rows, lower_rows], axis=0)
    square = jnp.dot(core, core.T, precision=HIGH)
    frame = jnp.eye(modes_count + fresh_count, modes_count, dtype=jnp.float32)
    for step in range(ITERS):
        frame = orthonormal(jnp.dot(square, frame, precision=HIGH))
    ritz = lax.optimization_barrier(jnp.sum(frame * jnp.dot(square, frame, precision=HIGH), axis=0))
    return (frame, jnp.sqrt(ritz))

def reference(basis, sigma, snapshots):
    modes_count = basis.shape[0]
    total = basis.shape[1] * 1.0
    first = inner(basis, snapshots, total)
    partial_value = snapshots - jnp.dot(first.T, basis, precision=HIGH)
    second = inner(basis, partial_value, total)
    residual = partial_value - jnp.dot(second.T, basis, precision=HIGH)
    gram = inner(residual, residual, total)
    lower = jnp.linalg.cholesky(gram)
    fresh = jax.scipy.linalg.solve_triangular(lower, residual, lower=True)
    frame, values = rotate(sigma, first + second, lower.T)
    modes = jnp.dot(frame[:modes_count].T, basis, precision=HIGH) + jnp.dot(frame[modes_count:].T, fresh, precision=HIGH)
    return (modes, values)
```

```python
import functools

import jax
import jax.numpy as jnp
from jax import lax
from jax.experimental import pallas as pl
from jax.experimental.pallas import tpu as pltpu
from jax.sharding import PartitionSpec as P

ITERS = 4
AXES = ("gx", "gy", "gz")
HIGH = lax.Precision.HIGHEST
NN = (((1,), (0,)), ((), ()))
NT = (((1,), (1,)), ((), ()))


def dot(a, b, dims=NN):
    return lax.dot_general(a, b, dims, precision=HIGH, preferred_element_type=jnp.float32)


def split(x):
    high = x.astype(jnp.bfloat16)
    return high, (x - high.astype(jnp.float32)).astype(jnp.bfloat16)


def blocks_of(columns, most):
    width = columns
    while width > most and width % 256 == 0:
        width //= 2
    return width


def gram_kernel(scale, steps, snap_ref, basis_ref, out_ref, acc_ref):
    step = pl.program_id(0)
    snap_high, snap_low = split(snap_ref[...])
    basis_high, basis_low = split(basis_ref[...])
    both = jnp.concatenate([snap_high, basis_high, snap_low, basis_low], axis=0)
    product = lax.dot_general(both, both, NT, preferred_element_type=jnp.float32)

    @pl.when(step == 0)
    def _():
        acc_ref[...] = product

    @pl.when(step > 0)
    def _():
        acc_ref[...] += product

    @pl.when(step == steps - 1)
    def _():
        count = out_ref.shape[0]
        total = acc_ref[...]
        rows = total[:count] + total[count:]
        out_ref[...] = (rows[:, :count] + rows[:, count:]) * scale


def gram(snapshots, basis, total):
    new, columns = snapshots.shape
    modes = basis.shape[0]
    width = blocks_of(columns, 2048)
    steps = columns // width
    count = new + modes
    return pl.pallas_call(
        functools.partial(gram_kernel, 1.0 / total, steps),
        out_shape=jax.ShapeDtypeStruct((count, count), jnp.float32),
        grid=(steps,),
        in_specs=[
            pl.BlockSpec((new, width), lambda i: (0, i)),
            pl.BlockSpec((modes, width), lambda i: (0, i)),
        ],
        out_specs=pl.BlockSpec((count, count), lambda i: (0, 0)),
        scratch_shapes=[pltpu.VMEM((2 * count, 2 * count), jnp.float32)],
        compiler_params=pltpu.CompilerParams(dimension_semantics=("arbitrary",)),
        name="gram",
    )(snapshots, basis)


def all_sum(x, sizes):
    for axis, size in sizes:
        if size & (size - 1):
            x = lax.psum(x, axis)
            continue
        bit = 1
        while bit < size:
            x = x + lax.ppermute(x, axis, [(i, i ^ bit) for i in range(size)])
            bit *= 2
    return x


def normalize(square, parts):
    n = square.shape[0]
    row = lax.broadcasted_iota(jnp.int32, (n, 1), 0)
    for j in range(n - 1):
        inverse = 1.0 / square[j : j + 1, j : j + 1]
        column = jnp.where(row > j, square[:, j : j + 1], 0.0)
        parts = [p - column * (p[j : j + 1] * inverse) for p in parts]
        square = square - column * (square[j : j + 1] * inverse)
    diagonal = lax.broadcasted_iota(jnp.int32, (n, n), 0) == lax.broadcasted_iota(jnp.int32, (n, n), 1)
    pivots = jnp.sum(jnp.where(diagonal, square, 0.0), axis=1, keepdims=True)
    scale = lax.rsqrt(pivots)
    return [p * scale for p in parts]


def update_kernel(
    width, sums_ref, sigma_ref, snap_ref, basis_ref, modes_ref, values_ref, data_ref, out_ref, step_ref, in_sem, out_sem
):
    modes = basis_ref.shape[0]
    new, columns = snap_ref.shape
    count = new + modes
    loads = [
        pltpu.make_async_copy(snap_ref, data_ref.at[pl.ds(0, new)], in_sem.at[0]),
        pltpu.make_async_copy(basis_ref, data_ref.at[pl.ds(new, modes)], in_sem.at[1]),
    ]
    for load in loads:
        load.start()

    gram_all = sums_ref[...]
    snap_gram = gram_all[:new, :new]
    first_t = gram_all[:new, new:]
    first = gram_all[new:, :new]
    corr = gram_all[new:, new:]
    joined = 2.0 * first - dot(corr, first)
    joined_t = 2.0 * first_t - dot(first_t, corr)
    rest = first_t - dot(joined_t, corr)
    residual = snap_gram - dot(joined_t, first) - dot(rest, joined)
    eye = (
        lax.broadcasted_iota(jnp.int32, (modes, modes), 0) == lax.broadcasted_iota(jnp.int32, (modes, modes), 1)
    )
    sigma_row = sigma_ref[...]
    sigma2 = sigma_row * sigma_row
    corner = jnp.where(eye, sigma2, 0.0) + dot(joined, joined_t)
    bend = dot(joined, residual)
    eye_new = (
        lax.broadcasted_iota(jnp.int32, (new, new), 0) == lax.broadcasted_iota(jnp.int32, (new, new), 1)
    ).astype(jnp.float32)

    half = step_ref.shape[1] // 2
    step_ref[...] = jnp.zeros_like(step_ref)
    step_ref[:modes, :modes] = corner
    step_ref[:modes, modes:count] = joined
    step_ref[:modes, half : half + modes] = corner
    step_ref[:modes, half + modes : half + count] = bend
    step_ref[modes:, :modes] = joined_t
    step_ref[modes:, modes:count] = eye_new
    step_ref[modes:, half : half + modes] = joined_t
    step_ref[modes:, half + modes : half + count] = residual

    left = step_ref[:modes, :half]
    right = step_ref[:modes, half:]
    for step in range(ITERS):
        if step:
            both = dot(right[:, :count], step_ref[...])
            left, right = both[:, :half], both[:, half:]
        for repeat in range(2):
            square = dot(left, right, NT)
            left, right = normalize(square, [left, right])

    after = dot(right[:, :count], step_ref[:, :half])
    lane = lax.broadcasted_iota(jnp.int32, (modes, half), 1)
    spread = jnp.concatenate([sigma_row, jnp.zeros((1, half - modes), jnp.float32)], axis=1)
    part = jnp.where(lane < modes, left * spread, jnp.where(lane < count, after, 0.0))
    ritz = dot(jnp.ones((8, half), jnp.float32), part * part, NT)
    values_ref[...] = jnp.sqrt(ritz[:1])

    y = left[:, :modes]
    z = left[:, modes:count]
    weights = jnp.concatenate([z, y - dot(z, joined_t)], axis=1)
    high, low = split(weights)
    left_side = jnp.concatenate(
        [jnp.concatenate([high, high], axis=1), jnp.concatenate([low, low], axis=1)], axis=0
    )
    for load in loads:
        load.wait()
    stores = []
    for i in range(columns // width):
        piece = pl.ds(i * width, width)
        data_high, data_low = split(data_ref[:, piece])
        data = jnp.concatenate([data_high, data_low], axis=0)
        product = lax.dot_general(left_side, data, NN, preferred_element_type=jnp.float32)
        out_ref[:, piece] = product[:modes] + product[modes:]
        store = pltpu.make_async_copy(out_ref.at[:, piece], modes_ref.at[:, piece], out_sem.at[i])
        store.start()
        stores.append(store)
    for store in stores:
        store.wait()


def update(sums, sigma, snapshots, basis):
    new, columns = snapshots.shape
    modes = basis.shape[0]
    count = new + modes
    width = blocks_of(columns, 2048)
    half = -(-count // 128) * 128
    return pl.pallas_call(
        functools.partial(update_kernel, width),
        out_shape=(
            jax.ShapeDtypeStruct((modes, columns), jnp.float32),
            jax.ShapeDtypeStruct((1, modes), jnp.float32),
        ),
        in_specs=[
            pl.BlockSpec(memory_space=pltpu.VMEM),
            pl.BlockSpec(memory_space=pltpu.VMEM),
            pl.BlockSpec(memory_space=pl.ANY),
            pl.BlockSpec(memory_space=pl.ANY),
        ],
        out_specs=(pl.BlockSpec(memory_space=pl.ANY), pl.BlockSpec(memory_space=pltpu.VMEM)),
        scratch_shapes=[
            pltpu.VMEM((count, columns), jnp.float32),
            pltpu.VMEM((modes, columns), jnp.float32),
            pltpu.VMEM((count, 2 * half), jnp.float32),
            pltpu.SemaphoreType.DMA((2,)),
            pltpu.SemaphoreType.DMA((columns // width,)),
        ],
        name="update",
    )(sums, sigma, snapshots, basis)


def per_device(sizes, basis, sigma, snapshots):
    total = basis.shape[1] * 1.0
    for _, size in sizes:
        total *= size
    sums = all_sum(gram(snapshots, basis, total), sizes)
    modes, values = update(sums, sigma.reshape(1, -1), snapshots, basis)
    return modes, values.reshape(-1)


def solution(mesh):
    placed = (P(None, AXES), P(), P(None, AXES))
    sizes = tuple((axis, mesh.shape[axis]) for axis in AXES)
    return jax.shard_map(
        functools.partial(per_device, sizes),
        mesh=mesh,
        in_specs=placed,
        out_specs=(P(None, AXES), P()),
        check_vma=False,
    )
```

```python
import functools

import jax
import jax.numpy as jnp
from jax import lax
from jax.experimental import pallas as pl
from jax.experimental.pallas import tpu as pltpu
from jax.sharding import PartitionSpec as P

ITERS = 4
AXES = ("gx", "gy", "gz")
HIGH = lax.Precision.HIGHEST
NN = (((1,), (0,)), ((), ()))
NT = (((1,), (1,)), ((), ()))


def dot(a, b, dims=NN):
    return lax.dot_general(a, b, dims, precision=HIGH, preferred_element_type=jnp.float32)


def split(x):
    high = x.astype(jnp.bfloat16)
    return high, (x - high.astype(jnp.float32)).astype(jnp.bfloat16)


def blocks_of(columns, most):
    width = columns
    while width > most and width % 256 == 0:
        width //= 2
    return width


def gram_kernel(scale, steps, snap_ref, basis_ref, out_ref, acc_ref):
    step = pl.program_id(0)
    snap_high, snap_low = split(snap_ref[...])
    basis_high, basis_low = split(basis_ref[...])
    both = jnp.concatenate([snap_high, basis_high, snap_low, basis_low], axis=0)
    product = lax.dot_general(both, both, NT, preferred_element_type=jnp.float32)

    @pl.when(step == 0)
    def _():
        acc_ref[...] = product

    @pl.when(step > 0)
    def _():
        acc_ref[...] += product

    @pl.when(step == steps - 1)
    def _():
        count = out_ref.shape[0]
        total = acc_ref[...]
        rows = total[:count] + total[count:]
        out_ref[...] = (rows[:, :count] + rows[:, count:]) * scale


def gram(snapshots, basis, total):
    new, columns = snapshots.shape
    modes = basis.shape[0]
    width = blocks_of(columns, 2048)
    steps = columns // width
    count = new + modes
    return pl.pallas_call(
        functools.partial(gram_kernel, 1.0 / total, steps),
        out_shape=jax.ShapeDtypeStruct((count, count), jnp.float32),
        grid=(steps,),
        in_specs=[
            pl.BlockSpec((new, width), lambda i: (0, i)),
            pl.BlockSpec((modes, width), lambda i: (0, i)),
        ],
        out_specs=pl.BlockSpec((count, count), lambda i: (0, 0)),
        scratch_shapes=[pltpu.VMEM((2 * count, 2 * count), jnp.float32)],
        compiler_params=pltpu.CompilerParams(dimension_semantics=("arbitrary",)),
        name="gram",
    )(snapshots, basis)


def all_sum(x, sizes):
    for axis, size in sizes:
        if size & (size - 1):
            x = lax.psum(x, axis)
            continue
        bit = 1
        while bit < size:
            x = x + lax.ppermute(x, axis, [(i, i ^ bit) for i in range(size)])
            bit *= 2
    return x


def normalize(square, parts):
    n, lanes = square.shape[0], parts[0].shape[1]
    groups = n // 8
    row = lax.broadcasted_iota(jnp.int32, (8, lanes), 0)
    parts = [[p[8 * q : 8 * q + 8] for q in range(groups)] for p in parts]
    spread = [
        [
            jnp.broadcast_to(square[8 * q : 8 * q + 8, l : l + 1], (8, lanes)) if q >= l // 8 else None
            for q in range(groups)
        ]
        for l in range(n)
    ]
    pivots = [jnp.ones((8, lanes), jnp.float32) for _ in range(groups)]
    for k in range(n):
        own, r = k // 8, k % 8
        column = spread[k]
        pivot = jnp.broadcast_to(column[own][r : r + 1], (8, lanes))
        pivots[own] = jnp.where(row == r, pivot, pivots[own])
        inverse = 1.0 / pivot
        for l in range(k + 1, n):
            entry = jnp.broadcast_to(column[l // 8][l % 8 : l % 8 + 1], (8, lanes))
            for q in range(l // 8, groups):
                if l == k + 1:
                    spread[l][q] = spread[l][q] - (column[q] * entry) * inverse
                else:
                    spread[l][q] = spread[l][q] - column[q] * (entry * inverse)
        for p in parts:
            line = jnp.broadcast_to(p[own][r : r + 1], (8, lanes)) * inverse
            for q in range(own, groups):
                if q > own:
                    p[q] = p[q] - column[q] * line
                elif r < 7:
                    p[q] = p[q] - jnp.where(row > r, column[q], 0.0) * line
    scales = [lax.rsqrt(p) for p in pivots]
    return [jnp.concatenate([x * s for x, s in zip(p, scales)], axis=0) for p in parts]


def update_kernel(
    width, sums_ref, sigma_ref, snap_ref, basis_ref, modes_ref, values_ref, data_ref, out_ref, step_ref, in_sem, out_sem
):
    modes = basis_ref.shape[0]
    new, columns = snap_ref.shape
    count = new + modes
    loads = [
        pltpu.make_async_copy(snap_ref, data_ref.at[pl.ds(0, new)], in_sem.at[0]),
        pltpu.make_async_copy(basis_ref, data_ref.at[pl.ds(new, modes)], in_sem.at[1]),
    ]
    for load in loads:
        load.start()

    gram_all = sums_ref[...]
    snap_gram = gram_all[:new, :new]
    first_t = gram_all[:new, new:]
    first = gram_all[new:, :new]
    corr = gram_all[new:, new:]
    joined = 2.0 * first - dot(corr, first)
    joined_t = 2.0 * first_t - dot(first_t, corr)
    rest = first_t - dot(joined_t, corr)
    residual = snap_gram - dot(joined_t, first) - dot(rest, joined)
    eye = (
        lax.broadcasted_iota(jnp.int32, (modes, modes), 0) == lax.broadcasted_iota(jnp.int32, (modes, modes), 1)
    )
    sigma_row = sigma_ref[...]
    sigma2 = sigma_row * sigma_row
    corner = jnp.where(eye, sigma2, 0.0) + dot(joined, joined_t)
    bend = dot(joined, residual)
    eye_new = (
        lax.broadcasted_iota(jnp.int32, (new, new), 0) == lax.broadcasted_iota(jnp.int32, (new, new), 1)
    ).astype(jnp.float32)

    half = step_ref.shape[1] // 2
    step_ref[...] = jnp.zeros_like(step_ref)
    step_ref[:modes, :modes] = corner
    step_ref[:modes, modes:count] = joined
    step_ref[:modes, half : half + modes] = corner
    step_ref[:modes, half + modes : half + count] = bend
    step_ref[modes:, :modes] = joined_t
    step_ref[modes:, modes:count] = eye_new
    step_ref[modes:, half : half + modes] = joined_t
    step_ref[modes:, half + modes : half + count] = residual

    left = step_ref[:modes, :half]
    right = step_ref[:modes, half:]
    for step in range(ITERS):
        if step:
            both = dot(right[:, :count], step_ref[...])
            left, right = both[:, :half], both[:, half:]
        for repeat in range(2):
            square = dot(left, right, NT)
            left, right = normalize(square, [left, right])

    after = dot(right[:, :count], step_ref[:, :half])
    lane = lax.broadcasted_iota(jnp.int32, (modes, half), 1)
    spread = jnp.concatenate([sigma_row, jnp.zeros((1, half - modes), jnp.float32)], axis=1)
    part = jnp.where(lane < modes, left * spread, jnp.where(lane < count, after, 0.0))
    ritz = dot(jnp.ones((8, half), jnp.float32), part * part, NT)
    values_ref[...] = jnp.sqrt(ritz[:1])

    y = left[:, :modes]
    z = left[:, modes:count]
    weights = jnp.concatenate([z, y - dot(z, joined_t)], axis=1)
    high, low = split(weights)
    left_side = jnp.concatenate(
        [jnp.concatenate([high, high], axis=1), jnp.concatenate([low, low], axis=1)], axis=0
    )
    for load in loads:
        load.wait()
    stores = []
    for i in range(columns // width):
        piece = pl.ds(i * width, width)
        data_high, data_low = split(data_ref[:, piece])
        data = jnp.concatenate([data_high, data_low], axis=0)
        product = lax.dot_general(left_side, data, NN, preferred_element_type=jnp.float32)
        out_ref[:, piece] = product[:modes] + product[modes:]
        store = pltpu.make_async_copy(out_ref.at[:, piece], modes_ref.at[:, piece], out_sem.at[i])
        store.start()
        stores.append(store)
    for store in stores:
        store.wait()


def update(sums, sigma, snapshots, basis):
    new, columns = snapshots.shape
    modes = basis.shape[0]
    count = new + modes
    width = blocks_of(columns, 2048)
    half = -(-count // 128) * 128
    return pl.pallas_call(
        functools.partial(update_kernel, width),
        out_shape=(
            jax.ShapeDtypeStruct((modes, columns), jnp.float32),
            jax.ShapeDtypeStruct((1, modes), jnp.float32),
        ),
        in_specs=[
            pl.BlockSpec(memory_space=pltpu.VMEM),
            pl.BlockSpec(memory_space=pltpu.VMEM),
            pl.BlockSpec(memory_space=pl.ANY),
            pl.BlockSpec(memory_space=pl.ANY),
        ],
        out_specs=(pl.BlockSpec(memory_space=pl.ANY), pl.BlockSpec(memory_space=pltpu.VMEM)),
        scratch_shapes=[
            pltpu.VMEM((count, columns), jnp.float32),
            pltpu.VMEM((modes, columns), jnp.float32),
            pltpu.VMEM((count, 2 * half), jnp.float32),
            pltpu.SemaphoreType.DMA((2,)),
            pltpu.SemaphoreType.DMA((columns // width,)),
        ],
        name="update",
    )(sums, sigma, snapshots, basis)


def per_device(sizes, basis, sigma, snapshots):
    total = basis.shape[1] * 1.0
    for _, size in sizes:
        total *= size
    sums = all_sum(gram(snapshots, basis, total), sizes)
    modes, values = update(sums, sigma.reshape(1, -1), snapshots, basis)
    return modes, values.reshape(-1)


def solution(mesh):
    placed = (P(None, AXES), P(), P(None, AXES))
    sizes = tuple((axis, mesh.shape[axis]) for axis in AXES)
    return jax.shard_map(
        functools.partial(per_device, sizes),
        mesh=mesh,
        in_specs=placed,
        out_specs=(P(None, AXES), P()),
        check_vma=False,
    )
```

```python
import functools

import jax
import jax.numpy as jnp
from jax import lax
from jax.experimental import pallas as pl
from jax.experimental.pallas import tpu as pltpu
from jax.sharding import PartitionSpec as P

ITERS = 4
GRAM_WIDTH = 4096
GRANT = 24 * 1024 * 1024
AXES = ("gx", "gy", "gz")
HIGH = lax.Precision.HIGHEST
NN = (((1,), (0,)), ((), ()))
NT = (((1,), (1,)), ((), ()))


def dot(a, b, dims=NN):
    return lax.dot_general(a, b, dims, precision=HIGH, preferred_element_type=jnp.float32)


def split(x):
    high = x.astype(jnp.bfloat16)
    return high, (x - high.astype(jnp.float32)).astype(jnp.bfloat16)


def blocks_of(columns, most):
    width = columns
    while width > most and width % 256 == 0:
        width //= 2
    return width


def gram_kernel(scale, width, snap_ref, basis_ref, out_ref, data_ref, sem):
    new, columns = snap_ref.shape
    modes = basis_ref.shape[0]
    count = new + modes
    steps = columns // width
    loads = []
    for i in range(steps):
        piece = pl.ds(i * width, width)
        pair = [
            pltpu.make_async_copy(snap_ref.at[:, piece], data_ref.at[pl.ds(0, new), piece], sem.at[0, i]),
            pltpu.make_async_copy(basis_ref.at[:, piece], data_ref.at[pl.ds(new, modes), piece], sem.at[1, i]),
        ]
        for load in pair:
            load.start()
        loads.append(pair)
    total = None
    for i in range(steps):
        for load in loads[i]:
            load.wait()
        both = jnp.concatenate(split(data_ref[:, pl.ds(i * width, width)]), axis=0)
        product = lax.dot_general(both, both, NT, preferred_element_type=jnp.float32)
        total = product if total is None else total + product
    rows = total[:count] + total[count:]
    out_ref[...] = (rows[:, :count] + rows[:, count:]) * scale


def gram(snapshots, basis, total):
    new, columns = snapshots.shape
    modes = basis.shape[0]
    width = blocks_of(columns, GRAM_WIDTH)
    count = new + modes
    return pl.pallas_call(
        functools.partial(gram_kernel, 1.0 / total, width),
        out_shape=jax.ShapeDtypeStruct((count, count), jnp.float32),
        in_specs=[pl.BlockSpec(memory_space=pltpu.HBM), pl.BlockSpec(memory_space=pltpu.HBM)],
        out_specs=pl.BlockSpec(memory_space=pltpu.VMEM),
        scratch_shapes=[
            pltpu.VMEM((count, columns), jnp.float32),
            pltpu.SemaphoreType.DMA((2, columns // width)),
        ],
        compiler_params=pltpu.CompilerParams(vmem_limit_bytes=GRANT),
        name="gram",
    )(snapshots, basis)


def all_sum(x, sizes):
    for axis, size in sizes:
        if size & (size - 1):
            x = lax.psum(x, axis)
            continue
        bit = 1
        while bit < size:
            x = x + lax.ppermute(x, axis, [(i, i ^ bit) for i in range(size)])
            bit *= 2
    return x


def normalize(square, parts):
    n, lanes = square.shape[0], parts[0].shape[1]
    groups = n // 8
    row = lax.broadcasted_iota(jnp.int32, (8, lanes), 0)
    parts = [[p[8 * q : 8 * q + 8] for q in range(groups)] for p in parts]
    spread = [
        [
            jnp.broadcast_to(square[8 * q : 8 * q + 8, l : l + 1], (8, lanes)) if q >= l // 8 else None
            for q in range(groups)
        ]
        for l in range(n)
    ]
    pivots = [jnp.ones((8, lanes), jnp.float32) for _ in range(groups)]
    for k in range(n):
        own, r = k // 8, k % 8
        column = spread[k]
        pivot = jnp.broadcast_to(column[own][r : r + 1], (8, lanes))
        pivots[own] = jnp.where(row == r, pivot, pivots[own])
        inverse = 1.0 / pivot
        for l in range(k + 1, n):
            entry = jnp.broadcast_to(column[l // 8][l % 8 : l % 8 + 1], (8, lanes))
            for q in range(l // 8, groups):
                if l == k + 1:
                    spread[l][q] = spread[l][q] - (column[q] * entry) * inverse
                else:
                    spread[l][q] = spread[l][q] - column[q] * (entry * inverse)
        for p in parts:
            line = jnp.broadcast_to(p[own][r : r + 1], (8, lanes)) * inverse
            for q in range(own, groups):
                if q > own:
                    p[q] = p[q] - column[q] * line
                elif r < 7:
                    p[q] = p[q] - jnp.where(row > r, column[q], 0.0) * line
    scales = [lax.rsqrt(p) for p in pivots]
    return [jnp.concatenate([x * s for x, s in zip(p, scales)], axis=0) for p in parts]


def update_kernel(
    width, sums_ref, sigma_ref, snap_ref, basis_ref, modes_ref, values_ref, data_ref, out_ref, step_ref, frame_ref, in_sem, out_sem
):
    modes = basis_ref.shape[0]
    new, columns = snap_ref.shape
    count = new + modes
    loads = [
        pltpu.make_async_copy(snap_ref, data_ref.at[pl.ds(0, new)], in_sem.at[0]),
        pltpu.make_async_copy(basis_ref, data_ref.at[pl.ds(new, modes)], in_sem.at[1]),
    ]
    for load in loads:
        load.start()

    gram_all = sums_ref[...]
    snap_gram = gram_all[:new, :new]
    first_t = gram_all[:new, new:]
    first = gram_all[new:, :new]
    corr = gram_all[new:, new:]
    joined = 2.0 * first - dot(corr, first)
    joined_t = 2.0 * first_t - dot(first_t, corr)
    rest = first_t - dot(joined_t, corr)
    residual = snap_gram - dot(joined_t, first) - dot(rest, joined)
    eye = (
        lax.broadcasted_iota(jnp.int32, (modes, modes), 0) == lax.broadcasted_iota(jnp.int32, (modes, modes), 1)
    )
    sigma_row = sigma_ref[...]
    sigma2 = sigma_row * sigma_row
    corner = jnp.where(eye, sigma2, 0.0) + dot(joined, joined_t)
    bend = dot(joined, residual)
    eye_new = (
        lax.broadcasted_iota(jnp.int32, (new, new), 0) == lax.broadcasted_iota(jnp.int32, (new, new), 1)
    ).astype(jnp.float32)

    half = step_ref.shape[1] // 2
    step_ref[...] = jnp.zeros_like(step_ref)
    step_ref[:modes, :modes] = corner
    step_ref[:modes, modes:count] = joined
    step_ref[:modes, half : half + modes] = corner
    step_ref[:modes, half + modes : half + count] = bend
    step_ref[modes:, :modes] = joined_t
    step_ref[modes:, modes:count] = eye_new
    step_ref[modes:, half : half + modes] = joined_t
    step_ref[modes:, half + modes : half + count] = residual

    def once(repeat, parts):
        return tuple(normalize(dot(*parts, NT), parts))

    def iterate(step, parts):
        left, right = lax.fori_loop(0, 2, once, parts)
        frame_ref[...] = left
        both = dot(right[:, :count], step_ref[...])
        return both[:, :half], both[:, half:]

    after, _ = lax.fori_loop(0, ITERS, iterate, (step_ref[:modes, :half], step_ref[:modes, half:]))
    left = frame_ref[...]
    lane = lax.broadcasted_iota(jnp.int32, (modes, half), 1)
    spread = jnp.concatenate([sigma_row, jnp.zeros((1, half - modes), jnp.float32)], axis=1)
    part = jnp.where(lane < modes, left * spread, jnp.where(lane < count, after, 0.0))
    ritz = dot(jnp.ones((8, half), jnp.float32), part * part, NT)
    values_ref[...] = jnp.sqrt(ritz[:1])

    y = left[:, :modes]
    z = left[:, modes:count]
    weights = jnp.concatenate([z, y - dot(z, joined_t)], axis=1)
    high, low = split(weights)
    left_side = jnp.concatenate(
        [jnp.concatenate([high, high], axis=1), jnp.concatenate([low, low], axis=1)], axis=0
    )
    for load in loads:
        load.wait()
    stores = []
    for i in range(columns // width):
        piece = pl.ds(i * width, width)
        data_high, data_low = split(data_ref[:, piece])
        data = jnp.concatenate([data_high, data_low], axis=0)
        product = lax.dot_general(left_side, data, NN, preferred_element_type=jnp.float32)
        out_ref[:, piece] = product[:modes] + product[modes:]
        store = pltpu.make_async_copy(out_ref.at[:, piece], modes_ref.at[:, piece], out_sem.at[i])
        store.start()
        stores.append(store)
    for store in stores:
        store.wait()


def update(sums, sigma, snapshots, basis):
    new, columns = snapshots.shape
    modes = basis.shape[0]
    count = new + modes
    width = blocks_of(columns, 2048)
    half = -(-count // 128) * 128
    return pl.pallas_call(
        functools.partial(update_kernel, width),
        out_shape=(
            jax.ShapeDtypeStruct((modes, columns), jnp.float32),
            jax.ShapeDtypeStruct((1, modes), jnp.float32),
        ),
        in_specs=[
            pl.BlockSpec(memory_space=pltpu.VMEM),
            pl.BlockSpec(memory_space=pltpu.VMEM),
            pl.BlockSpec(memory_space=pltpu.HBM),
            pl.BlockSpec(memory_space=pltpu.HBM),
        ],
        out_specs=(pl.BlockSpec(memory_space=pltpu.HBM), pl.BlockSpec(memory_space=pltpu.VMEM)),
        scratch_shapes=[
            pltpu.VMEM((count, columns), jnp.float32),
            pltpu.VMEM((modes, columns), jnp.float32),
            pltpu.VMEM((count, 2 * half), jnp.float32),
            pltpu.VMEM((modes, half), jnp.float32),
            pltpu.SemaphoreType.DMA((2,)),
            pltpu.SemaphoreType.DMA((columns // width,)),
        ],
        compiler_params=pltpu.CompilerParams(vmem_limit_bytes=GRANT),
        name="update",
    )(sums, sigma, snapshots, basis)


def per_device(sizes, basis, sigma, snapshots):
    total = basis.shape[1] * 1.0
    for _, size in sizes:
        total *= size
    basis = pltpu.with_memory_space_constraint(basis, pltpu.HBM)
    snapshots = pltpu.with_memory_space_constraint(snapshots, pltpu.HBM)
    sums = all_sum(gram(snapshots, basis, total), sizes)
    modes, values = update(sums, sigma.reshape(1, -1), snapshots, basis)
    return modes, values.reshape(-1)


def solution(mesh):
    placed = (P(None, AXES), P(), P(None, AXES))
    sizes = tuple((axis, mesh.shape[axis]) for axis in AXES)
    return jax.shard_map(
        functools.partial(per_device, sizes),
        mesh=mesh,
        in_specs=placed,
        out_specs=(P(None, AXES), P()),
        check_vma=False,
    )
```

```python
import functools

import jax
import jax.numpy as jnp
from jax import lax
from jax.experimental import pallas as pl
from jax.experimental.pallas import tpu as pltpu
from jax.sharding import PartitionSpec as P

ITERS = 4
GRAM_WIDTH = 4096
GRANT = 24 * 1024 * 1024
AXES = ("gx", "gy", "gz")
HIGH = lax.Precision.HIGHEST
NN = (((1,), (0,)), ((), ()))
NT = (((1,), (1,)), ((), ()))


def dot(a, b, dims=NN):
    return lax.dot_general(a, b, dims, precision=HIGH, preferred_element_type=jnp.float32)


def split(x):
    high = x.astype(jnp.bfloat16)
    return high, (x - high.astype(jnp.float32)).astype(jnp.bfloat16)


def blocks_of(columns, most):
    width = columns
    while width > most and width % 256 == 0:
        width //= 2
    return width


def gram_kernel(scale, width, snap_ref, basis_ref, out_ref, data_ref, sem):
    new, columns = snap_ref.shape
    modes = basis_ref.shape[0]
    count = new + modes
    steps = columns // width
    loads = []
    for i in range(steps):
        piece = pl.ds(i * width, width)
        pair = [
            pltpu.make_async_copy(snap_ref.at[:, piece], data_ref.at[pl.ds(0, new), piece], sem.at[0, i]),
            pltpu.make_async_copy(basis_ref.at[:, piece], data_ref.at[pl.ds(new, modes), piece], sem.at[1, i]),
        ]
        for load in pair:
            load.start()
        loads.append(pair)
    total = None
    for i in range(steps):
        for load in loads[i]:
            load.wait()
        both = jnp.concatenate(split(data_ref[:, pl.ds(i * width, width)]), axis=0)
        product = lax.dot_general(both, both, NT, preferred_element_type=jnp.float32)
        total = product if total is None else total + product
    rows = total[:count] + total[count:]
    out_ref[...] = (rows[:, :count] + rows[:, count:]) * scale


def gram(snapshots, basis, total):
    new, columns = snapshots.shape
    modes = basis.shape[0]
    width = blocks_of(columns, GRAM_WIDTH)
    count = new + modes
    return pl.pallas_call(
        functools.partial(gram_kernel, 1.0 / total, width),
        out_shape=jax.ShapeDtypeStruct((count, count), jnp.float32),
        in_specs=[pl.BlockSpec(memory_space=pltpu.HBM), pl.BlockSpec(memory_space=pltpu.HBM)],
        out_specs=pl.BlockSpec(memory_space=pltpu.VMEM),
        scratch_shapes=[
            pltpu.VMEM((count, columns), jnp.float32),
            pltpu.SemaphoreType.DMA((2, columns // width)),
        ],
        compiler_params=pltpu.CompilerParams(vmem_limit_bytes=GRANT),
        name="gram",
    )(snapshots, basis)


def all_sum(x, sizes):
    for axis, size in sizes:
        if size & (size - 1):
            x = lax.psum(x, axis)
            continue
        bit = 1
        while bit < size:
            x = x + lax.ppermute(x, axis, [(i, i ^ bit) for i in range(size)])
            bit *= 2
    return x


def normalize(square, parts):
    n, lanes = square.shape[0], parts[0].shape[1]
    groups = n // 8
    row = lax.broadcasted_iota(jnp.int32, (8, lanes), 0)
    parts = [[p[8 * q : 8 * q + 8] for q in range(groups)] for p in parts]
    spread = [
        [
            jnp.broadcast_to(square[8 * q : 8 * q + 8, l : l + 1], (8, lanes)) if q >= l // 8 else None
            for q in range(groups)
        ]
        for l in range(n)
    ]
    pivots = [jnp.ones((8, lanes), jnp.float32) for _ in range(groups)]
    for k in range(n):
        own, r = k // 8, k % 8
        column = spread[k]
        pivot = jnp.broadcast_to(column[own][r : r + 1], (8, lanes))
        pivots[own] = jnp.where(row == r, pivot, pivots[own])
        inverse = 1.0 / pivot
        scaled = [None if c is None else c * inverse for c in column]
        for l in range(k + 1, n):
            entry = jnp.broadcast_to(column[l // 8][l % 8 : l % 8 + 1], (8, lanes))
            for q in range(l // 8, groups):
                if l == k + 1:
                    spread[l][q] = spread[l][q] - (column[q] * entry) * inverse
                else:
                    spread[l][q] = spread[l][q] - scaled[q] * entry
        below = jnp.where(row > r, scaled[own], 0.0)
        for p in parts:
            line = jnp.broadcast_to(p[own][r : r + 1], (8, lanes))
            if r < 7:
                p[own] = p[own] - below * line
            for q in range(own + 1, groups):
                p[q] = p[q] - scaled[q] * line
    scales = [lax.rsqrt(p) for p in pivots]
    return [jnp.concatenate([x * s for x, s in zip(p, scales)], axis=0) for p in parts]


def update_kernel(
    width, sums_ref, sigma_ref, snap_ref, basis_ref, modes_ref, values_ref, data_ref, out_ref, step_ref, frame_ref, in_sem, out_sem
):
    modes = basis_ref.shape[0]
    new, columns = snap_ref.shape
    count = new + modes
    loads = [
        pltpu.make_async_copy(snap_ref, data_ref.at[pl.ds(0, new)], in_sem.at[0]),
        pltpu.make_async_copy(basis_ref, data_ref.at[pl.ds(new, modes)], in_sem.at[1]),
    ]
    for load in loads:
        load.start()

    half = step_ref.shape[1] // 2
    top = sums_ref[:new]
    low = sums_ref[new:]
    lane = lax.broadcasted_iota(jnp.int32, (modes, count), 1)
    on_modes = lane >= new
    diagonal = lane == new + lax.broadcasted_iota(jnp.int32, (modes, count), 0)
    wide = lax.broadcasted_iota(jnp.int32, (new, count), 1)
    unit = (wide == lax.broadcasted_iota(jnp.int32, (new, count), 0)).astype(jnp.float32)
    sigma = jnp.concatenate([jnp.zeros((1, new), jnp.float32), sigma_ref[...]], axis=1)

    def below(x):
        return jnp.concatenate([jnp.zeros((new, count), jnp.float32), x], axis=0)

    corr = jnp.where(on_modes, low, 0.0)
    twice = jnp.where(diagonal, 2.0, 0.0) - corr
    first = jnp.where(on_modes, 0.0, low)
    joined_t = dot(top, below(twice), NT)
    joined = dot(twice, below(first))
    rest = jnp.where(wide >= new, top, 0.0) - dot(joined_t, below(corr), NT)
    corner = jnp.where(diagonal, sigma * sigma, 0.0) + dot(joined, below(joined), NT)
    residual = jnp.where(wide >= new, 0.0, top) - dot(joined_t, below(first)) - dot(rest, below(joined))
    bend = dot(joined[:, :new], residual)

    step_ref[:, count:half] = jnp.zeros((count, half - count), jnp.float32)
    step_ref[:, half + count :] = jnp.zeros((count, half - count), jnp.float32)
    step_ref[:new, :count] = unit + joined_t
    step_ref[new:, :count] = joined + corner
    step_ref[:new, half : half + count] = residual + joined_t
    step_ref[new:, half : half + count] = bend + corner

    def iterate(step, parts):
        left, right = normalize(dot(*parts, NT), parts)
        after = dot(right[:, :count], step_ref[...])
        left, *after = normalize(dot(left, right, NT), [left, after[:, :half], after[:, half:]])
        frame_ref[...] = left
        return tuple(after)

    after, _ = lax.fori_loop(0, ITERS, iterate, (step_ref[new:, :half], step_ref[new:, half:]))
    left = frame_ref[:, :count]

    weights = left - dot(left[:, :new], joined_t)
    high, low_part = split(weights)
    left_side = jnp.concatenate(
        [jnp.concatenate([high, high], axis=1), jnp.concatenate([low_part, low_part], axis=1)], axis=0
    )
    for load in loads:
        load.wait()
    stores = []
    for i in range(columns // width):
        piece = pl.ds(i * width, width)
        data = jnp.concatenate(split(data_ref[:, piece]), axis=0)
        product = lax.dot_general(left_side, data, NN, preferred_element_type=jnp.float32)
        out_ref[:, piece] = product[:modes] + product[modes:]
        store = pltpu.make_async_copy(out_ref.at[:, piece], modes_ref.at[:, piece], out_sem.at[i])
        store.start()
        stores.append(store)

    part = jnp.where(on_modes, left * sigma, after[:, :count])
    values_ref[...] = jnp.sqrt(dot(jnp.ones((8, count), jnp.float32), part * part, NT)[:1])
    for store in stores:
        store.wait()


def update(sums, sigma, snapshots, basis):
    new, columns = snapshots.shape
    modes = basis.shape[0]
    count = new + modes
    width = blocks_of(columns, 2048)
    half = -(-count // 128) * 128
    return pl.pallas_call(
        functools.partial(update_kernel, width),
        out_shape=(
            jax.ShapeDtypeStruct((modes, columns), jnp.float32),
            jax.ShapeDtypeStruct((1, modes), jnp.float32),
        ),
        in_specs=[
            pl.BlockSpec(memory_space=pltpu.VMEM),
            pl.BlockSpec(memory_space=pltpu.VMEM),
            pl.BlockSpec(memory_space=pltpu.HBM),
            pl.BlockSpec(memory_space=pltpu.HBM),
        ],
        out_specs=(pl.BlockSpec(memory_space=pltpu.HBM), pl.BlockSpec(memory_space=pltpu.VMEM)),
        scratch_shapes=[
            pltpu.VMEM((count, columns), jnp.float32),
            pltpu.VMEM((modes, columns), jnp.float32),
            pltpu.VMEM((count, 2 * half), jnp.float32),
            pltpu.VMEM((modes, half), jnp.float32),
            pltpu.SemaphoreType.DMA((2,)),
            pltpu.SemaphoreType.DMA((columns // width,)),
        ],
        compiler_params=pltpu.CompilerParams(vmem_limit_bytes=GRANT),
        name="update",
    )(sums, sigma, snapshots, basis)


def per_device(sizes, basis, sigma, snapshots):
    total = basis.shape[1] * 1.0
    for _, size in sizes:
        total *= size
    basis = pltpu.with_memory_space_constraint(basis, pltpu.HBM)
    snapshots = pltpu.with_memory_space_constraint(snapshots, pltpu.HBM)
    sums = all_sum(gram(snapshots, basis, total), sizes)
    modes, values = update(sums, sigma.reshape(1, -1), snapshots, basis)
    return modes, values.reshape(-1)


def solution(mesh):
    placed = (P(None, AXES), P(), P(None, AXES))
    sizes = tuple((axis, mesh.shape[axis]) for axis in AXES)
    return jax.shard_map(
        functools.partial(per_device, sizes),
        mesh=mesh,
        in_specs=placed,
        out_specs=(P(None, AXES), P()),
        check_vma=False,
    )
```

```python
import functools

import jax
import jax.numpy as jnp
from jax import lax
from jax.experimental import pallas as pl
from jax.experimental.pallas import tpu as pltpu
from jax.sharding import PartitionSpec as P

ITERS = 4
GRAM_WIDTH = 4096
GRANT = 24 * 1024 * 1024
AXES = ("gx", "gy", "gz")
NN = (((1,), (0,)), ((), ()))
NT = (((1,), (1,)), ((), ()))


def pieces(x):
    high = x.astype(jnp.bfloat16)
    rest = x - high.astype(jnp.float32)
    middle = rest.astype(jnp.bfloat16)
    return high, middle, (rest - middle.astype(jnp.float32)).astype(jnp.bfloat16)


def as_left(x):
    high, middle, low = pieces(x)
    return jnp.concatenate([high, middle, high, low, middle, high], axis=1)


def as_right(x, axis):
    high, middle, low = pieces(x)
    return jnp.concatenate([high, high, middle, high, middle, low], axis=axis)


def product_of(left, right, dims=NN):
    return lax.dot_general(left, right, dims, preferred_element_type=jnp.float32)


def dot(a, b, dims=NN):
    return product_of(as_left(a), as_right(b, dims[0][1][0]), dims)


def split(x):
    high = x.astype(jnp.bfloat16)
    return high, (x - high.astype(jnp.float32)).astype(jnp.bfloat16)


def blocks_of(columns, most):
    width = columns
    while width > most and width % 256 == 0:
        width //= 2
    return width


def gram_kernel(scale, width, snap_ref, basis_ref, out_ref, data_ref, sem):
    new, columns = snap_ref.shape
    modes = basis_ref.shape[0]
    count = new + modes
    steps = columns // width
    loads = []
    for i in range(steps):
        piece = pl.ds(i * width, width)
        pair = [
            pltpu.make_async_copy(snap_ref.at[:, piece], data_ref.at[pl.ds(0, new), piece], sem.at[0, i]),
            pltpu.make_async_copy(basis_ref.at[:, piece], data_ref.at[pl.ds(new, modes), piece], sem.at[1, i]),
        ]
        for load in pair:
            load.start()
        loads.append(pair)
    total = None
    for i in range(steps):
        for load in loads[i]:
            load.wait()
        piece = pl.ds(i * width, width)
        snap, basis = split(data_ref[:new, piece]), split(data_ref[new:, piece])
        rows = jnp.concatenate([snap[0], basis[0], snap[1], basis[1]], axis=0)
        product = product_of(rows, rows, NT)
        total = product if total is None else total + product
    sent = out_ref.shape[1]
    rows = (total[:count] + total[count:]) * scale
    rows = rows[:, :count] + rows[:, count:]
    corr = jnp.concatenate([rows[new:, new:], jnp.zeros((new - modes, modes), jnp.float32)], axis=0)
    out_ref[...] = jnp.concatenate([rows[:new], corr], axis=1)


def gram(snapshots, basis, total):
    new, columns = snapshots.shape
    modes = basis.shape[0]
    width = blocks_of(columns, GRAM_WIDTH)
    count = new + modes
    return pl.pallas_call(
        functools.partial(gram_kernel, 1.0 / total, width),
        out_shape=jax.ShapeDtypeStruct((new, count + modes), jnp.float32),
        in_specs=[pl.BlockSpec(memory_space=pltpu.HBM), pl.BlockSpec(memory_space=pltpu.HBM)],
        out_specs=pl.BlockSpec(memory_space=pltpu.VMEM),
        scratch_shapes=[
            pltpu.VMEM((count, columns), jnp.float32),
            pltpu.SemaphoreType.DMA((2, columns // width)),
        ],
        compiler_params=pltpu.CompilerParams(vmem_limit_bytes=GRANT),
        name="gram",
    )(snapshots, basis)


def all_sum(x, sizes):
    for axis, size in sizes:
        if size & (size - 1):
            x = lax.psum(x, axis)
            continue
        bit = 1
        while bit < size:
            x = x + lax.ppermute(x, axis, [(i, i ^ bit) for i in range(size)])
            bit *= 2
    return x


def normalize(square, parts):
    n, lanes = square.shape[0], parts[0].shape[1]
    groups = n // 8
    row = lax.broadcasted_iota(jnp.int32, (8, lanes), 0)
    parts = [[p[8 * q : 8 * q + 8] for q in range(groups)] for p in parts]
    spread = [
        [
            jnp.broadcast_to(square[8 * q : 8 * q + 8, l : l + 1], (8, lanes)) if q >= l // 8 else None
            for q in range(groups)
        ]
        for l in range(n)
    ]
    pivots = [jnp.ones((8, lanes), jnp.float32) for _ in range(groups)]
    for k in range(n):
        own, r = k // 8, k % 8
        column = spread[k]
        pivot = jnp.broadcast_to(column[own][r : r + 1], (8, lanes))
        pivots[own] = jnp.where(row == r, pivot, pivots[own])
        inverse = 1.0 / pivot
        scaled = [None if c is None else c * inverse for c in column]
        for l in range(k + 1, n):
            entry = jnp.broadcast_to(column[l // 8][l % 8 : l % 8 + 1], (8, lanes))
            for q in range(l // 8, groups):
                if l == k + 1:
                    spread[l][q] = spread[l][q] - (column[q] * entry) * inverse
                else:
                    spread[l][q] = spread[l][q] - scaled[q] * entry
        below = jnp.where(row > r, scaled[own], 0.0)
        for p in parts:
            line = jnp.broadcast_to(p[own][r : r + 1], (8, lanes))
            if r < 7:
                p[own] = p[own] - below * line
            for q in range(own + 1, groups):
                p[q] = p[q] - scaled[q] * line
    scales = [lax.rsqrt(p) for p in pivots]
    return [jnp.concatenate([x * s for x, s in zip(p, scales)], axis=0) for p in parts]


def update_kernel(
    width, sums_ref, sigma_ref, snap_ref, basis_ref, modes_ref, values_ref, data_ref, out_ref, step_ref, frame_ref, in_sem, out_sem
):
    modes = basis_ref.shape[0]
    new, columns = snap_ref.shape
    count = new + modes
    loads = [
        pltpu.make_async_copy(snap_ref, data_ref.at[pl.ds(0, new)], in_sem.at[0]),
        pltpu.make_async_copy(basis_ref, data_ref.at[pl.ds(new, modes)], in_sem.at[1]),
    ]
    for load in loads:
        load.start()

    half = sums_ref.shape[1]
    top = sums_ref[...]
    lane = lax.broadcasted_iota(jnp.int32, (modes, half), 1)
    line = lax.broadcasted_iota(jnp.int32, (modes, half), 0)
    wide = lax.broadcasted_iota(jnp.int32, (new, half), 1)
    unit = (wide == lax.broadcasted_iota(jnp.int32, (new, half), 0)).astype(jnp.float32)
    sigma = jnp.concatenate(
        [jnp.zeros((1, new), jnp.float32), sigma_ref[...], jnp.zeros((1, half - count), jnp.float32)], axis=1
    )

    def at(place, x):
        above = [jnp.zeros((place, x.shape[1]), x.dtype)] if place else []
        under = half - place - x.shape[0]
        return jnp.concatenate(above + [x] + ([jnp.zeros((under, x.shape[1]), x.dtype)] if under else []), axis=0)

    corr = jnp.where(lane >= count, top[:modes], 0.0)
    same = jnp.where(lane == count + line, 1.0, 0.0)
    twice = 2.0 * same - corr
    pair = dot(jnp.where(wide < count, top, 0.0), at(new, jnp.concatenate([twice, same], axis=1)))
    joined_t, first_t = pair[:, :half], pair[:, half:]
    joined = dot(twice, at(0, first_t), NT)
    joined_at = dot(first_t, at(new, twice), NT)
    rest = first_t - dot(joined_t, at(count, corr))
    residual = (
        jnp.where(wide < new, top, 0.0) - dot(joined_t, at(0, first_t), NT) - dot(rest, at(0, joined_t), NT)
    )
    corner = jnp.where(lane == new + line, sigma * sigma, 0.0) + dot(joined, at(new, joined), NT)
    bend = dot(joined, at(0, residual))

    step = jnp.concatenate(
        [
            at(0, unit + joined_at) + at(new, joined + corner),
            at(0, residual + joined_at) + at(new, bend + corner),
        ],
        axis=1,
    )
    step_ref[...] = as_right(step, 0)

    def iterate(_, parts):
        left, right = normalize(dot(*parts, NT), parts)
        right = as_left(right)
        after = product_of(right, step_ref[...])
        high, middle, last = right[:, :half], right[:, half : 2 * half], right[:, 3 * half : 4 * half]
        square = product_of(as_left(left), jnp.concatenate([high, high, middle, high, middle, last], axis=1), NT)
        left, *after = normalize(square, [left, after[:, :half], after[:, half:]])
        frame_ref[...] = left
        return tuple(after)

    start = (joined + corner, bend + corner)
    after, _ = lax.fori_loop(0, ITERS, iterate, start)
    left = frame_ref[...]

    weights = (left - dot(left, at(0, joined_at)))[:, :count]
    high, low_part = split(weights)
    left_side = jnp.concatenate(
        [jnp.concatenate([high, high], axis=1), jnp.concatenate([low_part, low_part], axis=1)], axis=0
    )
    for load in loads:
        load.wait()
    stores = []
    for i in range(columns // width):
        piece = pl.ds(i * width, width)
        data = jnp.concatenate(split(data_ref[:, piece]), axis=0)
        product = lax.dot_general(left_side, data, NN, preferred_element_type=jnp.float32)
        out_ref[:, piece] = product[:modes] + product[modes:]
        store = pltpu.make_async_copy(out_ref.at[:, piece], modes_ref.at[:, piece], out_sem.at[i])
        store.start()
        stores.append(store)

    part = jnp.where(lane < new, after, left * sigma)
    values_ref[...] = jnp.sqrt(dot(jnp.ones((8, half), jnp.float32), part * part, NT)[:1])
    for store in stores:
        store.wait()


def update(sums, sigma, snapshots, basis):
    new, columns = snapshots.shape
    modes = basis.shape[0]
    count = new + modes
    width = blocks_of(columns, 2048)
    half = count + modes
    return pl.pallas_call(
        functools.partial(update_kernel, width),
        out_shape=(
            jax.ShapeDtypeStruct((modes, columns), jnp.float32),
            jax.ShapeDtypeStruct((1, modes), jnp.float32),
        ),
        in_specs=[
            pl.BlockSpec(memory_space=pltpu.VMEM),
            pl.BlockSpec(memory_space=pltpu.VMEM),
            pl.BlockSpec(memory_space=pltpu.HBM),
            pl.BlockSpec(memory_space=pltpu.HBM),
        ],
        out_specs=(pl.BlockSpec(memory_space=pltpu.HBM), pl.BlockSpec(memory_space=pltpu.VMEM)),
        scratch_shapes=[
            pltpu.VMEM((count, columns), jnp.float32),
            pltpu.VMEM((modes, columns), jnp.float32),
            pltpu.VMEM((6 * half, 2 * half), jnp.bfloat16),
            pltpu.VMEM((modes, half), jnp.float32),
            pltpu.SemaphoreType.DMA((2,)),
            pltpu.SemaphoreType.DMA((columns // width,)),
        ],
        compiler_params=pltpu.CompilerParams(vmem_limit_bytes=GRANT),
        name="update",
    )(sums, sigma, snapshots, basis)


def per_device(sizes, basis, sigma, snapshots):
    total = basis.shape[1] * 1.0
    for _, size in sizes:
        total *= size
    basis = pltpu.with_memory_space_constraint(basis, pltpu.HBM)
    snapshots = pltpu.with_memory_space_constraint(snapshots, pltpu.HBM)
    sums = all_sum(gram(snapshots, basis, total), sizes)
    modes, values = update(sums, sigma.reshape(1, -1), snapshots, basis)
    return modes, values.reshape(-1)


def solution(mesh):
    placed = (P(None, AXES), P(), P(None, AXES))
    sizes = tuple((axis, mesh.shape[axis]) for axis in AXES)
    return jax.shard_map(
        functools.partial(per_device, sizes),
        mesh=mesh,
        in_specs=placed,
        out_specs=(P(None, AXES), P()),
        check_vma=False,
    )
```

```python
import functools

import jax
import jax.numpy as jnp
from jax import lax
from jax.experimental import pallas as pl
from jax.experimental.pallas import tpu as pltpu
from jax.sharding import PartitionSpec as P

ITERS = 4
GRAM_WIDTH = 4096
GRANT = 24 * 1024 * 1024
AXES = ("gx", "gy", "gz")
NN = (((1,), (0,)), ((), ()))
NT = (((1,), (1,)), ((), ()))


def pieces(x):
    high = x.astype(jnp.bfloat16)
    rest = x - high.astype(jnp.float32)
    middle = rest.astype(jnp.bfloat16)
    return high, middle, (rest - middle.astype(jnp.float32)).astype(jnp.bfloat16)


def as_left(x):
    high, middle, low = pieces(x)
    return jnp.concatenate([high, middle, high, low, middle, high], axis=1)


def as_right(x, axis):
    high, middle, low = pieces(x)
    return jnp.concatenate([high, high, middle, high, middle, low], axis=axis)


def product_of(left, right, dims=NN):
    return lax.dot_general(left, right, dims, preferred_element_type=jnp.float32)


def dot(a, b, dims=NN):
    return product_of(as_left(a), as_right(b, dims[0][1][0]), dims)


def split(x):
    high = x.astype(jnp.bfloat16)
    return high, (x - high.astype(jnp.float32)).astype(jnp.bfloat16)


def blocks_of(columns, most):
    width = columns
    while width > most and width % 256 == 0:
        width //= 2
    return width


def gram_kernel(scale, width, snap_ref, basis_ref, out_ref, data_ref, sem):
    new, columns = snap_ref.shape
    modes = basis_ref.shape[0]
    count = new + modes
    steps = columns // width
    loads = []
    for i in range(steps):
        piece = pl.ds(i * width, width)
        pair = [
            pltpu.make_async_copy(snap_ref.at[:, piece], data_ref.at[pl.ds(0, new), piece], sem.at[0, i]),
            pltpu.make_async_copy(basis_ref.at[:, piece], data_ref.at[pl.ds(new, modes), piece], sem.at[1, i]),
        ]
        for load in pair:
            load.start()
        loads.append(pair)
    total = None
    for i in range(steps):
        for load in loads[i]:
            load.wait()
        piece = pl.ds(i * width, width)
        snap, basis = split(data_ref[:new, piece]), split(data_ref[new:, piece])
        rows = jnp.concatenate([snap[0], basis[0], snap[1], basis[1]], axis=0)
        product = product_of(rows, rows, NT)
        total = product if total is None else total + product
    sent = out_ref.shape[1]
    rows = (total[:count] + total[count:]) * scale
    rows = rows[:, :count] + rows[:, count:]
    part = modes // 2
    middle, last = rows[modes : modes + part], rows[modes + part : new]
    out_ref[...] = jnp.concatenate(
        [
            jnp.concatenate([rows[:modes], rows[new:, new:]], axis=1),
            jnp.concatenate([middle[:, modes:new], last[:, modes:new], middle[:, new:], last[:, new:]], axis=1),
        ],
        axis=0,
    )


def gram(snapshots, basis, total):
    new, columns = snapshots.shape
    modes = basis.shape[0]
    width = blocks_of(columns, GRAM_WIDTH)
    count = new + modes
    return pl.pallas_call(
        functools.partial(gram_kernel, 1.0 / total, width),
        out_shape=jax.ShapeDtypeStruct((modes + modes // 2, count + modes), jnp.float32),
        in_specs=[pl.BlockSpec(memory_space=pltpu.HBM), pl.BlockSpec(memory_space=pltpu.HBM)],
        out_specs=pl.BlockSpec(memory_space=pltpu.VMEM),
        scratch_shapes=[
            pltpu.VMEM((count, columns), jnp.float32),
            pltpu.SemaphoreType.DMA((2, columns // width)),
        ],
        compiler_params=pltpu.CompilerParams(vmem_limit_bytes=GRANT),
        name="gram",
    )(snapshots, basis)


def all_sum(x, sizes):
    for axis, size in sizes:
        if size & (size - 1):
            x = lax.psum(x, axis)
            continue
        bit = 1
        while bit < size:
            x = x + lax.ppermute(x, axis, [(i, i ^ bit) for i in range(size)])
            bit *= 2
    return x


def normalize(square, parts):
    n, lanes = square.shape[0], parts[0].shape[1]
    groups = n // 8
    row = lax.broadcasted_iota(jnp.int32, (8, lanes), 0)
    parts = [[p[8 * q : 8 * q + 8] for q in range(groups)] for p in parts]
    spread = [
        [
            jnp.broadcast_to(square[8 * q : 8 * q + 8, l : l + 1], (8, lanes)) if q >= l // 8 else None
            for q in range(groups)
        ]
        for l in range(n)
    ]
    pivots = [jnp.ones((8, lanes), jnp.float32) for _ in range(groups)]
    for k in range(n):
        own, r = k // 8, k % 8
        column = spread[k]
        pivot = jnp.broadcast_to(column[own][r : r + 1], (8, lanes))
        pivots[own] = jnp.where(row == r, pivot, pivots[own])
        inverse = 1.0 / pivot
        scaled = [None if c is None else c * inverse for c in column]
        for l in range(k + 1, n):
            entry = jnp.broadcast_to(column[l // 8][l % 8 : l % 8 + 1], (8, lanes))
            for q in range(l // 8, groups):
                if l == k + 1:
                    spread[l][q] = spread[l][q] - (column[q] * entry) * inverse
                else:
                    spread[l][q] = spread[l][q] - scaled[q] * entry
        below = jnp.where(row > r, scaled[own], 0.0)
        for p in parts:
            line = jnp.broadcast_to(p[own][r : r + 1], (8, lanes))
            if r < 7:
                p[own] = p[own] - below * line
            for q in range(own + 1, groups):
                p[q] = p[q] - scaled[q] * line
    scales = [lax.rsqrt(p) for p in pivots]
    return [jnp.concatenate([x * s for x, s in zip(p, scales)], axis=0) for p in parts]


def update_kernel(
    width, sums_ref, sigma_ref, snap_ref, basis_ref, modes_ref, values_ref, data_ref, out_ref, step_ref, frame_ref, in_sem, out_sem
):
    modes = basis_ref.shape[0]
    new, columns = snap_ref.shape
    count = new + modes
    loads = [
        pltpu.make_async_copy(snap_ref, data_ref.at[pl.ds(0, new)], in_sem.at[0]),
        pltpu.make_async_copy(basis_ref, data_ref.at[pl.ds(new, modes)], in_sem.at[1]),
    ]
    for load in loads:
        load.start()

    half = sums_ref.shape[1]
    upper = sums_ref[:modes]
    lower = sums_ref[modes:]
    cross = upper[:, modes:new]
    last = jnp.concatenate([lower[:, :modes], lower[:, modes:new]], axis=0)
    snap_gram = jnp.concatenate([upper[:, :new], jnp.concatenate([cross.T, last], axis=1)], axis=0)
    snap_gram = jnp.concatenate([snap_gram, jnp.zeros((new, half - new), jnp.float32)], axis=1)
    lane = lax.broadcasted_iota(jnp.int32, (modes, half), 1)
    line = lax.broadcasted_iota(jnp.int32, (modes, half), 0)
    wide = lax.broadcasted_iota(jnp.int32, (new, half), 1)
    unit = (wide == lax.broadcasted_iota(jnp.int32, (new, half), 0)).astype(jnp.float32)
    sigma = jnp.concatenate(
        [jnp.zeros((1, new), jnp.float32), sigma_ref[...], jnp.zeros((1, half - count), jnp.float32)], axis=1
    )

    def at(place, x):
        above = [jnp.zeros((place, x.shape[1]), x.dtype)] if place else []
        under = half - place - x.shape[0]
        return jnp.concatenate(above + [x] + ([jnp.zeros((under, x.shape[1]), x.dtype)] if under else []), axis=0)

    corr = jnp.where(lane >= count, upper, 0.0)
    same = jnp.where(lane == count + line, 1.0, 0.0)
    twice = 2.0 * same - corr
    sent = jnp.concatenate([upper, lower, lower], axis=0)
    late = lax.broadcasted_iota(jnp.int32, (new, half), 0) >= modes + modes // 2
    sent = jnp.where((wide >= new) & ((wide >= count) == late), sent, 0.0)
    both = jnp.concatenate([twice, same], axis=1)
    pair = dot(sent, jnp.concatenate([jnp.zeros((new, 2 * half), jnp.float32), both, both], axis=0))
    joined_t, first_t = pair[:, :half], pair[:, half:]
    joined = dot(twice, at(0, first_t), NT)
    joined_at = dot(first_t, at(new, twice), NT)
    rest = first_t - dot(joined_t, at(count, corr))
    residual = (
        snap_gram - dot(joined_t, at(0, first_t), NT) - dot(rest, at(0, joined_t), NT)
    )
    corner = jnp.where(lane == new + line, sigma * sigma, 0.0) + dot(joined, at(new, joined), NT)
    bend = dot(joined, at(0, residual))

    step = jnp.concatenate(
        [
            at(0, unit + joined_at) + at(new, joined + corner),
            at(0, residual + joined_at) + at(new, bend + corner),
        ],
        axis=1,
    )
    step_ref[...] = as_right(step, 0)

    def iterate(_, parts):
        left, right = normalize(dot(*parts, NT), parts)
        right = as_left(right)
        after = product_of(right, step_ref[...])
        high, middle, last = right[:, :half], right[:, half : 2 * half], right[:, 3 * half : 4 * half]
        square = product_of(as_left(left), jnp.concatenate([high, high, middle, high, middle, last], axis=1), NT)
        left, *after = normalize(square, [left, after[:, :half], after[:, half:]])
        frame_ref[...] = left
        return tuple(after)

    start = (joined + corner, bend + corner)
    after, _ = lax.fori_loop(0, ITERS, iterate, start)
    left = frame_ref[...]

    weights = (left - dot(left, at(0, joined_at)))[:, :count]
    high, low_part = split(weights)
    left_side = jnp.concatenate(
        [jnp.concatenate([high, high], axis=1), jnp.concatenate([low_part, low_part], axis=1)], axis=0
    )
    for load in loads:
        load.wait()
    stores = []
    for i in range(columns // width):
        piece = pl.ds(i * width, width)
        data = jnp.concatenate(split(data_ref[:, piece]), axis=0)
        product = lax.dot_general(left_side, data, NN, preferred_element_type=jnp.float32)
        out_ref[:, piece] = product[:modes] + product[modes:]
        store = pltpu.make_async_copy(out_ref.at[:, piece], modes_ref.at[:, piece], out_sem.at[i])
        store.start()
        stores.append(store)

    part = jnp.where(lane < new, after, left * sigma)
    values_ref[...] = jnp.sqrt(dot(jnp.ones((8, half), jnp.float32), part * part, NT)[:1])
    for store in stores:
        store.wait()


def update(sums, sigma, snapshots, basis):
    new, columns = snapshots.shape
    modes = basis.shape[0]
    count = new + modes
    width = blocks_of(columns, 1024)
    half = count + modes
    return pl.pallas_call(
        functools.partial(update_kernel, width),
        out_shape=(
            jax.ShapeDtypeStruct((modes, columns), jnp.float32),
            jax.ShapeDtypeStruct((1, modes), jnp.float32),
        ),
        in_specs=[
            pl.BlockSpec(memory_space=pltpu.VMEM),
            pl.BlockSpec(memory_space=pltpu.VMEM),
            pl.BlockSpec(memory_space=pltpu.HBM),
            pl.BlockSpec(memory_space=pltpu.HBM),
        ],
        out_specs=(pl.BlockSpec(memory_space=pltpu.HBM), pl.BlockSpec(memory_space=pltpu.VMEM)),
        scratch_shapes=[
            pltpu.VMEM((count, columns), jnp.float32),
            pltpu.VMEM((modes, columns), jnp.float32),
            pltpu.VMEM((6 * half, 2 * half), jnp.bfloat16),
            pltpu.VMEM((modes, half), jnp.float32),
            pltpu.SemaphoreType.DMA((2,)),
            pltpu.SemaphoreType.DMA((columns // width,)),
        ],
        compiler_params=pltpu.CompilerParams(vmem_limit_bytes=GRANT),
        name="update",
    )(sums, sigma, snapshots, basis)


def per_device(sizes, basis, sigma, snapshots):
    total = basis.shape[1] * 1.0
    for _, size in sizes:
        total *= size
    basis = pltpu.with_memory_space_constraint(basis, pltpu.HBM)
    snapshots = pltpu.with_memory_space_constraint(snapshots, pltpu.HBM)
    sums = all_sum(gram(snapshots, basis, total), sizes)
    modes, values = update(sums, sigma.reshape(1, -1), snapshots, basis)
    return modes, values.reshape(-1)


def solution(mesh):
    placed = (P(None, AXES), P(), P(None, AXES))
    sizes = tuple((axis, mesh.shape[axis]) for axis in AXES)
    return jax.shard_map(
        functools.partial(per_device, sizes),
        mesh=mesh,
        in_specs=placed,
        out_specs=(P(None, AXES), P()),
        check_vma=False,
    )
```

```python
import functools

import jax
import jax.numpy as jnp
from jax import lax
from jax.experimental import pallas as pl
from jax.experimental.pallas import tpu as pltpu
from jax.sharding import PartitionSpec as P

ITERS = 4
GRAM_WIDTH = 4096
GRANT = 24 * 1024 * 1024
AXES = ("gx", "gy", "gz")
NN = (((1,), (0,)), ((), ()))
NT = (((1,), (1,)), ((), ()))


def pieces(x):
    high = x.astype(jnp.bfloat16)
    rest = x - high.astype(jnp.float32)
    middle = rest.astype(jnp.bfloat16)
    return high, middle, (rest - middle.astype(jnp.float32)).astype(jnp.bfloat16)


def as_left(x):
    high, middle, low = pieces(x)
    return jnp.concatenate([high, middle, high, low, middle, high], axis=1)


def as_right(x, axis):
    high, middle, low = pieces(x)
    return jnp.concatenate([high, high, middle, high, middle, low], axis=axis)


def product_of(left, right, dims=NN):
    return lax.dot_general(left, right, dims, preferred_element_type=jnp.float32)


def dot(a, b, dims=NN):
    return product_of(as_left(a), as_right(b, dims[0][1][0]), dims)


def split(x):
    high = x.astype(jnp.bfloat16)
    return high, (x - high.astype(jnp.float32)).astype(jnp.bfloat16)


def blocks_of(columns, most):
    width = columns
    while width > most and width % 256 == 0:
        width //= 2
    return width


def gram_kernel(scale, width, snap_ref, basis_ref, out_ref, data_ref, sem):
    new, columns = snap_ref.shape
    modes = basis_ref.shape[0]
    count = new + modes
    steps = columns // width
    loads = []
    for i in range(steps):
        piece = pl.ds(i * width, width)
        pair = [
            pltpu.make_async_copy(snap_ref.at[:, piece], data_ref.at[pl.ds(0, new), piece], sem.at[0, i]),
            pltpu.make_async_copy(basis_ref.at[:, piece], data_ref.at[pl.ds(new, modes), piece], sem.at[1, i]),
        ]
        for load in pair:
            load.start()
        loads.append(pair)
    total = None
    for i in range(steps):
        for load in loads[i]:
            load.wait()
        piece = pl.ds(i * width, width)
        snap, basis = split(data_ref[:new, piece]), split(data_ref[new:, piece])
        rows = jnp.concatenate([snap[0], basis[0], snap[1], basis[1]], axis=0)
        product = product_of(rows, rows, NT)
        total = product if total is None else total + product
    sent = out_ref.shape[1]
    rows = (total[:count] + total[count:]) * scale
    rows = rows[:, :count] + rows[:, count:]
    part = modes // 2
    middle, last = rows[modes : modes + part], rows[modes + part : new]
    out_ref[...] = jnp.concatenate(
        [
            jnp.concatenate([rows[:modes], rows[new:, new:]], axis=1),
            jnp.concatenate([middle[:, modes:new], last[:, modes:new], middle[:, new:], last[:, new:]], axis=1),
        ],
        axis=0,
    )


def gram(snapshots, basis, total):
    new, columns = snapshots.shape
    modes = basis.shape[0]
    width = blocks_of(columns, GRAM_WIDTH)
    count = new + modes
    return pl.pallas_call(
        functools.partial(gram_kernel, 1.0 / total, width),
        out_shape=jax.ShapeDtypeStruct((modes + modes // 2, count + modes), jnp.float32),
        in_specs=[pl.BlockSpec(memory_space=pltpu.HBM), pl.BlockSpec(memory_space=pltpu.HBM)],
        out_specs=pl.BlockSpec(memory_space=pltpu.VMEM),
        scratch_shapes=[
            pltpu.VMEM((count, columns), jnp.float32),
            pltpu.SemaphoreType.DMA((2, columns // width)),
        ],
        compiler_params=pltpu.CompilerParams(vmem_limit_bytes=GRANT),
        name="gram",
    )(snapshots, basis)


def all_sum(x, sizes):
    for axis, size in sizes:
        if size & (size - 1):
            x = lax.psum(x, axis)
            continue
        bit = 1
        while bit < size:
            x = x + lax.ppermute(x, axis, [(i, i ^ bit) for i in range(size)])
            bit *= 2
    return x


def normalize(square, parts):
    n, lanes = square.shape[0], parts[0].shape[1]
    groups, late = n // 8, min(n, 16)
    row = lax.broadcasted_iota(jnp.int32, (8, lanes), 0)
    parts = [[p[8 * q : 8 * q + 8] for q in range(groups)] for p in parts]
    square = [square[8 * q : 8 * q + 8] for q in range(groups)]

    def spread_of(l):
        return [jnp.broadcast_to(square[q][:, l : l + 1], (8, lanes)) if q >= l // 8 else None for q in range(groups)]

    spread = [spread_of(l) if l < late else None for l in range(n)]
    pivots = [jnp.ones((8, lanes), jnp.float32) for _ in range(groups)]
    for k in range(n):
        own, r = k // 8, k % 8
        if k == 8:
            for l in range(late, n):
                spread[l] = spread_of(l)
        column = spread[k]
        pivot = jnp.broadcast_to(column[own][r : r + 1], (8, lanes))
        pivots[own] = jnp.where(row == r, column[own], pivots[own])
        inverse = 1.0 / pivot
        scaled = [None if c is None else c * inverse for c in column]
        for l in range(k + 1, n if k >= 8 else late):
            entry = jnp.broadcast_to(column[l // 8][l % 8 : l % 8 + 1], (8, lanes))
            for q in range(l // 8, groups):
                if l == k + 1:
                    spread[l][q] = spread[l][q] - (column[q] * entry) * inverse
                else:
                    spread[l][q] = spread[l][q] - scaled[q] * entry
        below = jnp.where(row > r, scaled[own], 0.0)
        if k < 8:
            line = jnp.broadcast_to(square[0][r : r + 1], (8, n))
            for q in [0] * (r < 7) + list(range(late // 8, groups)):
                square[q] = square[q] - (below if q == 0 else scaled[q])[:, :n] * line
        for p in parts:
            line = jnp.broadcast_to(p[own][r : r + 1], (8, lanes))
            if r < 7:
                p[own] = p[own] - below * line
            for q in range(own + 1, groups):
                p[q] = p[q] - scaled[q] * line
    scales = [lax.rsqrt(p) for p in pivots]
    return [jnp.concatenate([x * s for x, s in zip(p, scales)], axis=0) for p in parts]


def update_kernel(
    width, sums_ref, sigma_ref, snap_ref, basis_ref, modes_ref, values_ref, data_ref, out_ref, step_ref, frame_ref, in_sem, out_sem
):
    modes = basis_ref.shape[0]
    new, columns = snap_ref.shape
    count = new + modes
    loads = [
        pltpu.make_async_copy(snap_ref, data_ref.at[pl.ds(0, new)], in_sem.at[0]),
        pltpu.make_async_copy(basis_ref, data_ref.at[pl.ds(new, modes)], in_sem.at[1]),
    ]
    for load in loads:
        load.start()

    half = sums_ref.shape[1]
    upper = sums_ref[:modes]
    lower = sums_ref[modes:]
    cross = upper[:, modes:new]
    last = jnp.concatenate([lower[:, :modes], lower[:, modes:new]], axis=0)
    snap_gram = jnp.concatenate([upper[:, :new], jnp.concatenate([cross.T, last], axis=1)], axis=0)
    snap_gram = jnp.concatenate([snap_gram, jnp.zeros((new, half - new), jnp.float32)], axis=1)
    lane = lax.broadcasted_iota(jnp.int32, (modes, half), 1)
    line = lax.broadcasted_iota(jnp.int32, (modes, half), 0)
    wide = lax.broadcasted_iota(jnp.int32, (new, half), 1)
    unit = (wide == lax.broadcasted_iota(jnp.int32, (new, half), 0)).astype(jnp.float32)
    sigma = jnp.concatenate(
        [jnp.zeros((1, new), jnp.float32), sigma_ref[...], jnp.zeros((1, half - count), jnp.float32)], axis=1
    )

    def at(place, x):
        above = [jnp.zeros((place, x.shape[1]), x.dtype)] if place else []
        under = half - place - x.shape[0]
        return jnp.concatenate(above + [x] + ([jnp.zeros((under, x.shape[1]), x.dtype)] if under else []), axis=0)

    corr = jnp.where(lane >= count, upper, 0.0)
    same = jnp.where(lane == count + line, 1.0, 0.0)
    twice = 2.0 * same - corr
    sent = jnp.concatenate([upper, lower, lower], axis=0)
    late = lax.broadcasted_iota(jnp.int32, (new, half), 0) >= modes + modes // 2
    sent = jnp.where((wide >= new) & ((wide >= count) == late), sent, 0.0)
    both = jnp.concatenate([twice, same], axis=1)
    pair = dot(sent, jnp.concatenate([jnp.zeros((new, 2 * half), jnp.float32), both, both], axis=0))
    joined_t, first_t = pair[:, :half], pair[:, half:]
    joined = dot(twice, at(0, first_t), NT)
    joined_at = dot(first_t, at(new, twice), NT)
    rest = first_t - dot(joined_t, at(count, corr))
    residual = (
        snap_gram - dot(joined_t, at(0, first_t), NT) - dot(rest, at(0, joined_t), NT)
    )
    corner = jnp.where(lane == new + line, sigma * sigma, 0.0) + dot(joined, at(new, joined), NT)
    bend = dot(joined, at(0, residual))

    step = jnp.concatenate(
        [
            at(0, unit + joined_at) + at(new, joined + corner),
            at(0, residual + joined_at) + at(new, bend + corner),
        ],
        axis=1,
    )
    step_ref[...] = as_right(step, 0)

    def iterate(_, parts):
        left, right = normalize(dot(*parts, NT), parts)
        right = as_left(right)
        after = product_of(right, step_ref[...])
        high, middle, last = right[:, :half], right[:, half : 2 * half], right[:, 3 * half : 4 * half]
        square = product_of(as_left(left), jnp.concatenate([high, high, middle, high, middle, last], axis=1), NT)
        left, *after = normalize(square, [left, after[:, :half], after[:, half:]])
        frame_ref[...] = left
        return tuple(after)

    start = (joined + corner, bend + corner)
    after, _ = lax.fori_loop(0, ITERS, iterate, start)
    left = frame_ref[...]

    weights = (left - dot(left, at(0, joined_at)))[:, :count]
    high, low_part = split(weights)
    left_side = jnp.concatenate(
        [jnp.concatenate([high, high], axis=1), jnp.concatenate([low_part, low_part], axis=1)], axis=0
    )
    for load in loads:
        load.wait()
    stores = []
    for i in range(columns // width):
        piece = pl.ds(i * width, width)
        data = jnp.concatenate(split(data_ref[:, piece]), axis=0)
        product = lax.dot_general(left_side, data, NN, preferred_element_type=jnp.float32)
        out_ref[:, piece] = product[:modes] + product[modes:]
        store = pltpu.make_async_copy(out_ref.at[:, piece], modes_ref.at[:, piece], out_sem.at[i])
        store.start()
        stores.append(store)

    part = jnp.where(lane < new, after, left * sigma)
    values_ref[...] = jnp.sqrt(dot(jnp.ones((8, half), jnp.float32), part * part, NT)[:1])
    for store in stores:
        store.wait()


def update(sums, sigma, snapshots, basis):
    new, columns = snapshots.shape
    modes = basis.shape[0]
    count = new + modes
    width = blocks_of(columns, 1024)
    half = count + modes
    return pl.pallas_call(
        functools.partial(update_kernel, width),
        out_shape=(
            jax.ShapeDtypeStruct((modes, columns), jnp.float32),
            jax.ShapeDtypeStruct((1, modes), jnp.float32),
        ),
        in_specs=[
            pl.BlockSpec(memory_space=pltpu.VMEM),
            pl.BlockSpec(memory_space=pltpu.VMEM),
            pl.BlockSpec(memory_space=pltpu.HBM),
            pl.BlockSpec(memory_space=pltpu.HBM),
        ],
        out_specs=(pl.BlockSpec(memory_space=pltpu.HBM), pl.BlockSpec(memory_space=pltpu.VMEM)),
        scratch_shapes=[
            pltpu.VMEM((count, columns), jnp.float32),
            pltpu.VMEM((modes, columns), jnp.float32),
            pltpu.VMEM((6 * half, 2 * half), jnp.bfloat16),
            pltpu.VMEM((modes, half), jnp.float32),
            pltpu.SemaphoreType.DMA((2,)),
            pltpu.SemaphoreType.DMA((columns // width,)),
        ],
        compiler_params=pltpu.CompilerParams(vmem_limit_bytes=GRANT),
        name="update",
    )(sums, sigma, snapshots, basis)


def per_device(sizes, basis, sigma, snapshots):
    total = basis.shape[1] * 1.0
    for _, size in sizes:
        total *= size
    basis = pltpu.with_memory_space_constraint(basis, pltpu.HBM)
    snapshots = pltpu.with_memory_space_constraint(snapshots, pltpu.HBM)
    sums = all_sum(gram(snapshots, basis, total), sizes)
    modes, values = update(sums, sigma.reshape(1, -1), snapshots, basis)
    return modes, values.reshape(-1)


def solution(mesh):
    placed = (P(None, AXES), P(), P(None, AXES))
    sizes = tuple((axis, mesh.shape[axis]) for axis in AXES)
    return jax.shard_map(
        functools.partial(per_device, sizes),
        mesh=mesh,
        in_specs=placed,
        out_specs=(P(None, AXES), P()),
        check_vma=False,
    )
```

```python
import functools

import jax
import jax.numpy as jnp
from jax import lax
from jax.experimental import pallas as pl
from jax.experimental.pallas import tpu as pltpu
from jax.sharding import PartitionSpec as P

ITERS = 4
LEAD = 8
GRAM_WIDTH = 4096
GRANT = 24 * 1024 * 1024
AXES = ("gx", "gy", "gz")
NN = (((1,), (0,)), ((), ()))
NT = (((1,), (1,)), ((), ()))


def pieces(x):
    high = x.astype(jnp.bfloat16)
    rest = x - high.astype(jnp.float32)
    middle = rest.astype(jnp.bfloat16)
    return high, middle, (rest - middle.astype(jnp.float32)).astype(jnp.bfloat16)


def as_left(x):
    high, middle, low = pieces(x)
    return jnp.concatenate([high, middle, high, low, middle, high], axis=1)


def as_right(x, axis):
    high, middle, low = pieces(x)
    return jnp.concatenate([high, high, middle, high, middle, low], axis=axis)


def product_of(left, right, dims=NN):
    return lax.dot_general(left, right, dims, preferred_element_type=jnp.float32)


def dot(a, b, dims=NN):
    return product_of(as_left(a), as_right(b, dims[0][1][0]), dims)


def split(x):
    high = x.astype(jnp.bfloat16)
    return high, (x - high.astype(jnp.float32)).astype(jnp.bfloat16)


def blocks_of(columns, most):
    width = columns
    while width > most and width % 256 == 0:
        width //= 2
    return width


def gram_kernel(scale, width, snap_ref, basis_ref, out_ref, data_ref, sem):
    new, columns = snap_ref.shape
    modes = basis_ref.shape[0]
    count = new + modes
    steps = columns // width
    loads = []
    for i in range(steps):
        piece = pl.ds(i * width, width)
        pair = [
            pltpu.make_async_copy(snap_ref.at[:, piece], data_ref.at[pl.ds(0, new), piece], sem.at[0, i]),
            pltpu.make_async_copy(basis_ref.at[:, piece], data_ref.at[pl.ds(new, modes), piece], sem.at[1, i]),
        ]
        for load in pair:
            load.start()
        loads.append(pair)
    total = None
    for i in range(steps):
        for load in loads[i]:
            load.wait()
        piece = pl.ds(i * width, width)
        snap, basis = split(data_ref[:new, piece]), split(data_ref[new:, piece])
        rows = jnp.concatenate([snap[0], basis[0], snap[1], basis[1]], axis=0)
        product = product_of(rows, rows, NT)
        total = product if total is None else total + product
    sent = out_ref.shape[1]
    rows = (total[:count] + total[count:]) * scale
    rows = rows[:, :count] + rows[:, count:]
    part = modes // 2
    middle, last = rows[modes : modes + part], rows[modes + part : new]
    out_ref[...] = jnp.concatenate(
        [
            jnp.concatenate([rows[:modes], rows[new:, new:]], axis=1),
            jnp.concatenate([middle[:, modes:new], last[:, modes:new], middle[:, new:], last[:, new:]], axis=1),
        ],
        axis=0,
    )


def gram(snapshots, basis, total):
    new, columns = snapshots.shape
    modes = basis.shape[0]
    width = blocks_of(columns, GRAM_WIDTH)
    count = new + modes
    return pl.pallas_call(
        functools.partial(gram_kernel, 1.0 / total, width),
        out_shape=jax.ShapeDtypeStruct((modes + modes // 2, count + modes), jnp.float32),
        in_specs=[pl.BlockSpec(memory_space=pltpu.HBM), pl.BlockSpec(memory_space=pltpu.HBM)],
        out_specs=pl.BlockSpec(memory_space=pltpu.VMEM),
        scratch_shapes=[
            pltpu.VMEM((count, columns), jnp.float32),
            pltpu.SemaphoreType.DMA((2, columns // width)),
        ],
        compiler_params=pltpu.CompilerParams(vmem_limit_bytes=GRANT),
        name="gram",
    )(snapshots, basis)


def all_sum(x, sizes):
    for axis, size in sizes:
        if size & (size - 1):
            x = lax.psum(x, axis)
            continue
        bit = 1
        while bit < size:
            x = x + lax.ppermute(x, axis, [(i, i ^ bit) for i in range(size)])
            bit *= 2
    return x


def normalize(left, right, others):
    n, lanes = left.shape
    groups = n // 8
    row = lax.broadcasted_iota(jnp.int32, (8, lanes), 0)
    parts = [[p[8 * q : 8 * q + 8] for q in range(groups)] for p in (left, *others)]

    def start(l):
        return max(0, l // 8 * 8 - LEAD)

    def column_of(l):
        line = jnp.broadcast_to(right[l : l + 1], (8, lanes))
        return [
            jnp.broadcast_to(jnp.sum(parts[0][q] * line, axis=1, keepdims=True), (8, lanes)) if q >= l // 8 else None
            for q in range(groups)
        ]

    spread = [None] * n
    pivots = [jnp.ones((8, lanes), jnp.float32) for _ in range(groups)]
    for k in range(n):
        own, r = k // 8, k % 8
        for l in range(k, n):
            if start(l) == k:
                spread[l] = column_of(l)
        column = spread[k]
        pivots[own] = jnp.where(row == r, column[own], pivots[own])
        inverse = 1.0 / jnp.broadcast_to(column[own][r : r + 1], (8, lanes))
        scaled = [None if c is None else c * inverse for c in column]
        for l in range(k + 1, n):
            if start(l) > k:
                continue
            entry = jnp.broadcast_to(column[l // 8][l % 8 : l % 8 + 1], (8, lanes))
            for q in range(l // 8, groups):
                if l == k + 1:
                    spread[l][q] = spread[l][q] - (column[q] * entry) * inverse
                else:
                    spread[l][q] = spread[l][q] - scaled[q] * entry
        below = jnp.where(row > r, scaled[own], 0.0)
        for p in parts:
            line = jnp.broadcast_to(p[own][r : r + 1], (8, lanes))
            if r < 7:
                p[own] = p[own] - below * line
            for q in range(own + 1, groups):
                p[q] = p[q] - scaled[q] * line
    scales = [lax.rsqrt(p) for p in pivots]
    return [jnp.concatenate([x * s for x, s in zip(p, scales)], axis=0) for p in parts]


def update_kernel(
    width, sums_ref, sigma_ref, snap_ref, basis_ref, modes_ref, values_ref, data_ref, out_ref, step_ref, frame_ref, in_sem, out_sem
):
    modes = basis_ref.shape[0]
    new, columns = snap_ref.shape
    count = new + modes
    loads = [
        pltpu.make_async_copy(snap_ref, data_ref.at[pl.ds(0, new)], in_sem.at[0]),
        pltpu.make_async_copy(basis_ref, data_ref.at[pl.ds(new, modes)], in_sem.at[1]),
    ]
    for load in loads:
        load.start()

    half = sums_ref.shape[1]
    upper = sums_ref[:modes]
    lower = sums_ref[modes:]
    cross = upper[:, modes:new]
    last = jnp.concatenate([lower[:, :modes], lower[:, modes:new]], axis=0)
    snap_gram = jnp.concatenate([upper[:, :new], jnp.concatenate([cross.T, last], axis=1)], axis=0)
    snap_gram = jnp.concatenate([snap_gram, jnp.zeros((new, half - new), jnp.float32)], axis=1)
    lane = lax.broadcasted_iota(jnp.int32, (modes, half), 1)
    line = lax.broadcasted_iota(jnp.int32, (modes, half), 0)
    wide = lax.broadcasted_iota(jnp.int32, (new, half), 1)
    unit = (wide == lax.broadcasted_iota(jnp.int32, (new, half), 0)).astype(jnp.float32)
    sigma = jnp.concatenate(
        [jnp.zeros((1, new), jnp.float32), sigma_ref[...], jnp.zeros((1, half - count), jnp.float32)], axis=1
    )

    def at(place, x):
        above = [jnp.zeros((place, x.shape[1]), x.dtype)] if place else []
        under = half - place - x.shape[0]
        return jnp.concatenate(above + [x] + ([jnp.zeros((under, x.shape[1]), x.dtype)] if under else []), axis=0)

    corr = jnp.where(lane >= count, upper, 0.0)
    same = jnp.where(lane == count + line, 1.0, 0.0)
    twice = 2.0 * same - corr
    sent = jnp.concatenate([upper, lower, lower], axis=0)
    late = lax.broadcasted_iota(jnp.int32, (new, half), 0) >= modes + modes // 2
    sent = jnp.where((wide >= new) & ((wide >= count) == late), sent, 0.0)
    both = jnp.concatenate([twice, same], axis=1)
    pair = dot(sent, jnp.concatenate([jnp.zeros((new, 2 * half), jnp.float32), both, both], axis=0))
    joined_t, first_t = pair[:, :half], pair[:, half:]
    joined = dot(twice, at(0, first_t), NT)
    joined_at = dot(first_t, at(new, twice), NT)
    rest = first_t - dot(joined_t, at(count, corr))
    residual = (
        snap_gram - dot(joined_t, at(0, first_t), NT) - dot(rest, at(0, joined_t), NT)
    )
    corner = jnp.where(lane == new + line, sigma * sigma, 0.0) + dot(joined, at(new, joined), NT)
    bend = dot(joined, at(0, residual))

    step = jnp.concatenate(
        [
            at(0, unit + joined_at) + at(new, joined + corner),
            at(0, residual + joined_at) + at(new, bend + corner),
        ],
        axis=1,
    )
    step_ref[...] = as_right(step, 0)

    def iterate(_, parts):
        left, right = normalize(*parts, [parts[1]])
        after = product_of(as_left(right), step_ref[...])
        left, *after = normalize(left, right, [after[:, :half], after[:, half:]])
        frame_ref[...] = left
        return tuple(after)

    start = (joined + corner, bend + corner)
    after, _ = lax.fori_loop(0, ITERS, iterate, start)
    left = frame_ref[...]

    weights = (left - dot(left, at(0, joined_at)))[:, :count]
    high, low_part = split(weights)
    left_side = jnp.concatenate(
        [jnp.concatenate([high, high], axis=1), jnp.concatenate([low_part, low_part], axis=1)], axis=0
    )
    for load in loads:
        load.wait()
    stores = []
    for i in range(columns // width):
        piece = pl.ds(i * width, width)
        data = jnp.concatenate(split(data_ref[:, piece]), axis=0)
        product = lax.dot_general(left_side, data, NN, preferred_element_type=jnp.float32)
        out_ref[:, piece] = product[:modes] + product[modes:]
        store = pltpu.make_async_copy(out_ref.at[:, piece], modes_ref.at[:, piece], out_sem.at[i])
        store.start()
        stores.append(store)

    part = jnp.where(lane < new, after, left * sigma)
    values_ref[...] = jnp.sqrt(dot(jnp.ones((8, half), jnp.float32), part * part, NT)[:1])
    for store in stores:
        store.wait()


def update(sums, sigma, snapshots, basis):
    new, columns = snapshots.shape
    modes = basis.shape[0]
    count = new + modes
    width = blocks_of(columns, 1024)
    half = count + modes
    return pl.pallas_call(
        functools.partial(update_kernel, width),
        out_shape=(
            jax.ShapeDtypeStruct((modes, columns), jnp.float32),
            jax.ShapeDtypeStruct((1, modes), jnp.float32),
        ),
        in_specs=[
            pl.BlockSpec(memory_space=pltpu.VMEM),
            pl.BlockSpec(memory_space=pltpu.VMEM),
            pl.BlockSpec(memory_space=pltpu.HBM),
            pl.BlockSpec(memory_space=pltpu.HBM),
        ],
        out_specs=(pl.BlockSpec(memory_space=pltpu.HBM), pl.BlockSpec(memory_space=pltpu.VMEM)),
        scratch_shapes=[
            pltpu.VMEM((count, columns), jnp.float32),
            pltpu.VMEM((modes, columns), jnp.float32),
            pltpu.VMEM((6 * half, 2 * half), jnp.bfloat16),
            pltpu.VMEM((modes, half), jnp.float32),
            pltpu.SemaphoreType.DMA((2,)),
            pltpu.SemaphoreType.DMA((columns // width,)),
        ],
        compiler_params=pltpu.CompilerParams(vmem_limit_bytes=GRANT),
        name="update",
    )(sums, sigma, snapshots, basis)


def per_device(sizes, basis, sigma, snapshots):
    total = basis.shape[1] * 1.0
    for _, size in sizes:
        total *= size
    basis = pltpu.with_memory_space_constraint(basis, pltpu.HBM)
    snapshots = pltpu.with_memory_space_constraint(snapshots, pltpu.HBM)
    sums = all_sum(gram(snapshots, basis, total), sizes)
    modes, values = update(sums, sigma.reshape(1, -1), snapshots, basis)
    return modes, values.reshape(-1)


def solution(mesh):
    placed = (P(None, AXES), P(), P(None, AXES))
    sizes = tuple((axis, mesh.shape[axis]) for axis in AXES)
    return jax.shard_map(
        functools.partial(per_device, sizes),
        mesh=mesh,
        in_specs=placed,
        out_specs=(P(None, AXES), P()),
        check_vma=False,
    )
```

```python
import functools

import jax
import jax.numpy as jnp
from jax import lax
from jax.experimental import pallas as pl
from jax.experimental.pallas import tpu as pltpu
from jax.sharding import PartitionSpec as P

ITERS = 4
LEAD = 8
GRAM_WIDTH = 4096
GRANT = 24 * 1024 * 1024
AXES = ("gx", "gy", "gz")
NN = (((1,), (0,)), ((), ()))
NT = (((1,), (1,)), ((), ()))


def pieces(x):
    high = x.astype(jnp.bfloat16)
    rest = x - high.astype(jnp.float32)
    middle = rest.astype(jnp.bfloat16)
    return high, middle, (rest - middle.astype(jnp.float32)).astype(jnp.bfloat16)


def as_left(x):
    high, middle, low = pieces(x)
    return jnp.concatenate([high, middle, high, low, middle, high], axis=1)


def as_right(x, axis):
    high, middle, low = pieces(x)
    return jnp.concatenate([high, high, middle, high, middle, low], axis=axis)


def product_of(left, right, dims=NN):
    return lax.dot_general(left, right, dims, preferred_element_type=jnp.float32)


def dot(a, b, dims=NN):
    return product_of(as_left(a), as_right(b, dims[0][1][0]), dims)


def split(x):
    high = x.astype(jnp.bfloat16)
    return high, (x - high.astype(jnp.float32)).astype(jnp.bfloat16)


def blocks_of(columns, most):
    width = columns
    while width > most and width % 256 == 0:
        width //= 2
    return width


def gram_kernel(scale, width, snap_ref, basis_ref, out_ref, data_ref, sem):
    new, columns = snap_ref.shape
    modes = basis_ref.shape[0]
    count = new + modes
    steps = columns // width
    loads = []
    for i in range(steps):
        piece = pl.ds(i * width, width)
        pair = [
            pltpu.make_async_copy(snap_ref.at[:, piece], data_ref.at[pl.ds(0, new), piece], sem.at[0, i]),
            pltpu.make_async_copy(basis_ref.at[:, piece], data_ref.at[pl.ds(new, modes), piece], sem.at[1, i]),
        ]
        for load in pair:
            load.start()
        loads.append(pair)
    total = None
    for i in range(steps):
        for load in loads[i]:
            load.wait()
        piece = pl.ds(i * width, width)
        snap, basis = split(data_ref[:new, piece]), split(data_ref[new:, piece])
        rows = jnp.concatenate([snap[0], basis[0], snap[1], basis[1]], axis=0)
        product = product_of(rows, rows, NT)
        total = product if total is None else total + product
    sent = out_ref.shape[1]
    rows = (total[:count] + total[count:]) * scale
    rows = rows[:, :count] + rows[:, count:]
    part = modes // 2
    middle, last = rows[modes : modes + part], rows[modes + part : new]
    out_ref[...] = jnp.concatenate(
        [
            jnp.concatenate([rows[:modes], rows[new:, new:]], axis=1),
            jnp.concatenate([middle[:, modes:new], last[:, modes:new], middle[:, new:], last[:, new:]], axis=1),
        ],
        axis=0,
    )


def gram(snapshots, basis, total):
    new, columns = snapshots.shape
    modes = basis.shape[0]
    width = blocks_of(columns, GRAM_WIDTH)
    count = new + modes
    return pl.pallas_call(
        functools.partial(gram_kernel, 1.0 / total, width),
        out_shape=jax.ShapeDtypeStruct((modes + modes // 2, count + modes), jnp.float32),
        in_specs=[pl.BlockSpec(memory_space=pltpu.HBM), pl.BlockSpec(memory_space=pltpu.HBM)],
        out_specs=pl.BlockSpec(memory_space=pltpu.VMEM),
        scratch_shapes=[
            pltpu.VMEM((count, columns), jnp.float32),
            pltpu.SemaphoreType.DMA((2, columns // width)),
        ],
        compiler_params=pltpu.CompilerParams(vmem_limit_bytes=GRANT),
        name="gram",
    )(snapshots, basis)


def all_sum(x, sizes):
    for axis, size in sizes:
        if size & (size - 1):
            x = lax.psum(x, axis)
            continue
        bit = 1
        while bit < size:
            x = x + lax.ppermute(x, axis, [(i, i ^ bit) for i in range(size)])
            bit *= 2
    return x


def normalize(left, right, others):
    n, lanes = left.shape
    groups = n // 8
    row = lax.broadcasted_iota(jnp.int32, (8, lanes), 0)
    parts = [[p[8 * q : 8 * q + 8] for q in range(groups)] for p in (left, *others)]

    def start(l):
        return max(0, l // 8 * 8 - LEAD)

    def column_of(l):
        line = jnp.broadcast_to(right[l : l + 1], (8, lanes))
        return [
            jnp.broadcast_to(jnp.sum(parts[0][q] * line, axis=1, keepdims=True), (8, lanes)) if q >= l // 8 else None
            for q in range(groups)
        ]

    spread = [None] * n
    pivots = [jnp.ones((8, lanes), jnp.float32) for _ in range(groups)]
    for k in range(n):
        own, r = k // 8, k % 8
        for l in range(k, n):
            if start(l) == k:
                spread[l] = column_of(l)
        column = spread[k]
        pivots[own] = jnp.where(row == r, column[own], pivots[own])
        inverse = 1.0 / jnp.broadcast_to(column[own][r : r + 1], (8, lanes))
        scaled = [None if c is None else c * inverse for c in column]
        for l in range(k + 1, n):
            if start(l) > k:
                continue
            entry = jnp.broadcast_to(column[l // 8][l % 8 : l % 8 + 1], (8, lanes))
            for q in range(l // 8, groups):
                if l == k + 1:
                    spread[l][q] = spread[l][q] - (column[q] * entry) * inverse
                else:
                    spread[l][q] = spread[l][q] - scaled[q] * entry
        below = jnp.where(row > r, scaled[own], 0.0)
        for p in parts:
            line = jnp.broadcast_to(p[own][r : r + 1], (8, lanes))
            if r < 7:
                p[own] = p[own] - below * line
            for q in range(own + 1, groups):
                p[q] = p[q] - scaled[q] * line
    scales = [lax.rsqrt(p) for p in pivots]
    return [jnp.concatenate([x * s for x, s in zip(p, scales)], axis=0) for p in parts]


def update_kernel(
    width, sums_ref, sigma_ref, snap_ref, basis_ref, modes_ref, values_ref, data_ref, out_ref, step_ref, frame_ref, in_sem, out_sem
):
    modes = basis_ref.shape[0]
    new, columns = snap_ref.shape
    count = new + modes
    loads = [
        pltpu.make_async_copy(snap_ref, data_ref.at[pl.ds(0, new)], in_sem.at[0]),
        pltpu.make_async_copy(basis_ref, data_ref.at[pl.ds(new, modes)], in_sem.at[1]),
    ]
    for load in loads:
        load.start()

    half = sums_ref.shape[1]
    upper = sums_ref[:modes]
    lower = sums_ref[modes:]
    cross = upper[:, modes:new]
    last = jnp.concatenate([lower[:, :modes], lower[:, modes:new]], axis=0)
    snap_gram = jnp.concatenate([upper[:, :new], jnp.concatenate([cross.T, last], axis=1)], axis=0)
    snap_gram = jnp.concatenate([snap_gram, jnp.zeros((new, half - new), jnp.float32)], axis=1)
    lane = lax.broadcasted_iota(jnp.int32, (modes, half), 1)
    line = lax.broadcasted_iota(jnp.int32, (modes, half), 0)
    wide = lax.broadcasted_iota(jnp.int32, (new, half), 1)
    unit = (wide == lax.broadcasted_iota(jnp.int32, (new, half), 0)).astype(jnp.float32)
    sigma = jnp.concatenate([jnp.zeros((1, count), jnp.float32), sigma_ref[...]], axis=1)
    early = jnp.concatenate([jnp.zeros((1, new), jnp.float32), sigma_ref[...], jnp.zeros((1, modes), jnp.float32)], axis=1)

    def at(place, x):
        above = [jnp.zeros((place, x.shape[1]), x.dtype)] if place else []
        under = half - place - x.shape[0]
        return jnp.concatenate(above + [x] + ([jnp.zeros((under, x.shape[1]), x.dtype)] if under else []), axis=0)

    corr = jnp.where(lane >= count, upper, 0.0)
    same = jnp.where(lane == count + line, 1.0, 0.0)
    twice = 2.0 * same - corr
    sent = jnp.concatenate([upper, lower, lower], axis=0)
    late = lax.broadcasted_iota(jnp.int32, (new, half), 0) >= modes + modes // 2
    sent = jnp.where((wide >= new) & ((wide >= count) == late), sent, 0.0)
    above = jnp.zeros((new, half), jnp.float32)
    joined_t = dot(sent, jnp.concatenate([above, twice, twice], axis=0))
    pick = jnp.concatenate([above, same, same], axis=0).astype(jnp.bfloat16)
    first_t = product_of(jnp.concatenate(pieces(sent), axis=1), jnp.concatenate([pick] * 3, axis=0))
    joined = dot(twice, at(0, first_t), NT)
    rest = first_t - dot(joined_t, at(count, corr))
    residual = (
        snap_gram - dot(joined_t, at(0, first_t), NT) - dot(rest, at(0, joined_t), NT)
    )
    corner = jnp.where(lane == count + line, sigma * sigma, 0.0) + dot(joined, at(count, joined), NT)
    scaling = jnp.where(lane == new + line, early * early, 0.0)
    bend = dot(joined, at(0, residual))

    step = jnp.concatenate(
        [
            at(0, unit + joined_t) + at(count, joined + scaling + corner),
            at(0, residual + joined_t) + at(count, bend + corner),
        ],
        axis=1,
    )
    step_ref[...] = as_right(step, 0)

    def iterate(_, parts):
        left, right = normalize(*parts, [parts[1]])
        after = product_of(as_left(right), step_ref[...])
        left, *after = normalize(left, right, [after[:, :half], after[:, half:]])
        frame_ref[...] = left
        return tuple(after)

    start = (joined + scaling + corner, bend + corner)
    after, _ = lax.fori_loop(0, ITERS, iterate, start)
    left = frame_ref[...]

    high, low_part = split(left[:, :count])
    left_side = jnp.concatenate(
        [jnp.concatenate([high, high], axis=1), jnp.concatenate([low_part, low_part], axis=1)], axis=0
    )
    for load in loads:
        load.wait()
    stores = []
    for i in range(columns // width):
        piece = pl.ds(i * width, width)
        data = jnp.concatenate(split(data_ref[:, piece]), axis=0)
        product = lax.dot_general(left_side, data, NN, preferred_element_type=jnp.float32)
        out_ref[:, piece] = product[:modes] + product[modes:]
        store = pltpu.make_async_copy(out_ref.at[:, piece], modes_ref.at[:, piece], out_sem.at[i])
        store.start()
        stores.append(store)

    part = jnp.where(lane < new, after, left * sigma)
    values_ref[...] = jnp.sqrt(dot(jnp.ones((8, half), jnp.float32), part * part, NT)[:1])
    for store in stores:
        store.wait()


def update(sums, sigma, snapshots, basis):
    new, columns = snapshots.shape
    modes = basis.shape[0]
    count = new + modes
    width = blocks_of(columns, 1024)
    half = count + modes
    return pl.pallas_call(
        functools.partial(update_kernel, width),
        out_shape=(
            jax.ShapeDtypeStruct((modes, columns), jnp.float32),
            jax.ShapeDtypeStruct((1, modes), jnp.float32),
        ),
        in_specs=[
            pl.BlockSpec(memory_space=pltpu.VMEM),
            pl.BlockSpec(memory_space=pltpu.VMEM),
            pl.BlockSpec(memory_space=pltpu.HBM),
            pl.BlockSpec(memory_space=pltpu.HBM),
        ],
        out_specs=(pl.BlockSpec(memory_space=pltpu.HBM), pl.BlockSpec(memory_space=pltpu.VMEM)),
        scratch_shapes=[
            pltpu.VMEM((count, columns), jnp.float32),
            pltpu.VMEM((modes, columns), jnp.float32),
            pltpu.VMEM((6 * half, 2 * half), jnp.bfloat16),
            pltpu.VMEM((modes, half), jnp.float32),
            pltpu.SemaphoreType.DMA((2,)),
            pltpu.SemaphoreType.DMA((columns // width,)),
        ],
        compiler_params=pltpu.CompilerParams(vmem_limit_bytes=GRANT),
        name="update",
    )(sums, sigma, snapshots, basis)


def per_device(sizes, basis, sigma, snapshots):
    total = basis.shape[1] * 1.0
    for _, size in sizes:
        total *= size
    basis = pltpu.with_memory_space_constraint(basis, pltpu.HBM)
    snapshots = pltpu.with_memory_space_constraint(snapshots, pltpu.HBM)
    sums = all_sum(gram(snapshots, basis, total), sizes)
    modes, values = update(sums, sigma.reshape(1, -1), snapshots, basis)
    return modes, values.reshape(-1)


def solution(mesh):
    placed = (P(None, AXES), P(), P(None, AXES))
    sizes = tuple((axis, mesh.shape[axis]) for axis in AXES)
    return jax.shard_map(
        functools.partial(per_device, sizes),
        mesh=mesh,
        in_specs=placed,
        out_specs=(P(None, AXES), P()),
        check_vma=False,
    )
```

```python
import functools

import jax
import jax.numpy as jnp
from jax import lax
from jax.experimental import pallas as pl
from jax.experimental.pallas import tpu as pltpu
from jax.sharding import PartitionSpec as P

ITERS = 4
LEAD = 8
GRAM_WIDTH = 4096
GRANT = 24 * 1024 * 1024
AXES = ("gx", "gy", "gz")
NN = (((1,), (0,)), ((), ()))
NT = (((1,), (1,)), ((), ()))


def pieces(x):
    high = x.astype(jnp.bfloat16)
    rest = x - high.astype(jnp.float32)
    middle = rest.astype(jnp.bfloat16)
    return high, middle, (rest - middle.astype(jnp.float32)).astype(jnp.bfloat16)


def as_left(x):
    high, middle, low = pieces(x)
    return jnp.concatenate([high, middle, high, low, middle, high], axis=1)


def as_right(x, axis):
    high, middle, low = pieces(x)
    return jnp.concatenate([high, high, middle, high, middle, low], axis=axis)


def product_of(left, right, dims=NN):
    return lax.dot_general(left, right, dims, preferred_element_type=jnp.float32)


def dot(a, b, dims=NN):
    return product_of(as_left(a), as_right(b, dims[0][1][0]), dims)


def split(x):
    high = x.astype(jnp.bfloat16)
    return high, (x - high.astype(jnp.float32)).astype(jnp.bfloat16)


def blocks_of(columns, most):
    width = columns
    while width > most and width % 256 == 0:
        width //= 2
    return width


def gram_kernel(scale, width, snap_ref, basis_ref, out_ref, data_ref, sem):
    new, columns = snap_ref.shape
    modes = basis_ref.shape[0]
    count = new + modes
    steps = columns // width
    loads = []
    for i in range(steps):
        piece = pl.ds(i * width, width)
        pair = [
            pltpu.make_async_copy(snap_ref.at[:, piece], data_ref.at[pl.ds(0, new), piece], sem.at[0, i]),
            pltpu.make_async_copy(basis_ref.at[:, piece], data_ref.at[pl.ds(new, modes), piece], sem.at[1, i]),
        ]
        for load in pair:
            load.start()
        loads.append(pair)
    total = None
    for i in range(steps):
        for load in loads[i]:
            load.wait()
        piece = pl.ds(i * width, width)
        snap, basis = split(data_ref[:new, piece]), split(data_ref[new:, piece])
        rows = jnp.concatenate([snap[0], basis[0], snap[1], basis[1]], axis=0)
        lanes = jnp.concatenate([snap[0], basis[0], basis[1], snap[1]], axis=0)
        product = product_of(rows, lanes, NT)
        total = product if total is None else total + product
    rows = (total[:count] + total[count:]) * scale
    sent = out_ref.shape[1]
    squares = rows[:, :sent] + jnp.concatenate([rows[:, sent:], jnp.zeros((count, sent - new), jnp.float32)], axis=1)
    left = rows[:, :sent] + pltpu.roll(rows[:, :sent], sent - modes, 1)
    right = rows[:, :sent] + pltpu.roll(rows[:, :sent], modes, 1)
    part = modes // 2
    lane = lax.broadcasted_iota(jnp.int32, (modes, sent), 1)
    out_ref[:modes] = jnp.where(lane < new, squares[:modes], jnp.where(lane < count, left[:modes], right[new:]))
    lane = lane[:part]
    middle, last = slice(modes, modes + part), slice(modes + part, new)
    moved = pltpu.roll(squares[middle], sent - modes, 1)
    out_ref[modes:] = jnp.where(
        lane < modes,
        moved,
        jnp.where(lane < new, squares[last], jnp.where(lane < count, left[middle], right[last])),
    )


def gram(snapshots, basis, total):
    new, columns = snapshots.shape
    modes = basis.shape[0]
    width = blocks_of(columns, GRAM_WIDTH)
    count = new + modes
    return pl.pallas_call(
        functools.partial(gram_kernel, 1.0 / total, width),
        out_shape=jax.ShapeDtypeStruct((modes + modes // 2, count + modes), jnp.float32),
        in_specs=[pl.BlockSpec(memory_space=pltpu.HBM), pl.BlockSpec(memory_space=pltpu.HBM)],
        out_specs=pl.BlockSpec(memory_space=pltpu.VMEM),
        scratch_shapes=[
            pltpu.VMEM((count, columns), jnp.float32),
            pltpu.SemaphoreType.DMA((2, columns // width)),
        ],
        compiler_params=pltpu.CompilerParams(vmem_limit_bytes=GRANT),
        name="gram",
    )(snapshots, basis)


def all_sum(x, sizes):
    for axis, size in sizes:
        if size & (size - 1):
            x = lax.psum(x, axis)
            continue
        bit = 1
        while bit < size:
            x = x + lax.ppermute(x, axis, [(i, i ^ bit) for i in range(size)])
            bit *= 2
    return x


def normalize(left, right, others):
    n, lanes = left.shape
    groups = n // 8
    row = lax.broadcasted_iota(jnp.int32, (8, lanes), 0)
    parts = [[p[8 * q : 8 * q + 8] for q in range(groups)] for p in (left, *others)]

    def start(l):
        return max(0, l // 8 * 8 - LEAD)

    def column_of(l):
        line = jnp.broadcast_to(right[l : l + 1], (8, lanes))
        return [
            jnp.broadcast_to(jnp.sum(parts[0][q] * line, axis=1, keepdims=True), (8, lanes)) if q >= l // 8 else None
            for q in range(groups)
        ]

    spread = [None] * n
    pivots = [jnp.ones((8, lanes), jnp.float32) for _ in range(groups)]
    for k in range(n):
        own, r = k // 8, k % 8
        for l in range(k, n):
            if start(l) == k:
                spread[l] = column_of(l)
        column = spread[k]
        pivots[own] = jnp.where(row == r, column[own], pivots[own])
        inverse = 1.0 / jnp.broadcast_to(column[own][r : r + 1], (8, lanes))
        scaled = [None if c is None else c * inverse for c in column]
        for l in range(k + 1, n):
            if start(l) > k:
                continue
            entry = jnp.broadcast_to(column[l // 8][l % 8 : l % 8 + 1], (8, lanes))
            for q in range(l // 8, groups):
                if l == k + 1:
                    spread[l][q] = spread[l][q] - (column[q] * entry) * inverse
                else:
                    spread[l][q] = spread[l][q] - scaled[q] * entry
        below = jnp.where(row > r, scaled[own], 0.0)
        for p in parts:
            line = jnp.broadcast_to(p[own][r : r + 1], (8, lanes))
            if r < 7:
                p[own] = p[own] - below * line
            for q in range(own + 1, groups):
                p[q] = p[q] - scaled[q] * line
    scales = [lax.rsqrt(p) for p in pivots]
    return [jnp.concatenate([x * s for x, s in zip(p, scales)], axis=0) for p in parts]


def update_kernel(
    width, sums_ref, sigma_ref, snap_ref, basis_ref, modes_ref, values_ref, data_ref, out_ref, step_ref, frame_ref, in_sem, out_sem
):
    modes = basis_ref.shape[0]
    new, columns = snap_ref.shape
    count = new + modes
    loads = [
        pltpu.make_async_copy(snap_ref, data_ref.at[pl.ds(0, new)], in_sem.at[0]),
        pltpu.make_async_copy(basis_ref, data_ref.at[pl.ds(new, modes)], in_sem.at[1]),
    ]
    for load in loads:
        load.start()

    half = sums_ref.shape[1]
    upper = sums_ref[:modes]
    lower = sums_ref[modes:]
    cross = upper[:, modes:new]
    last = jnp.concatenate([lower[:, :modes], lower[:, modes:new]], axis=0)
    snap_gram = jnp.concatenate([upper[:, :new], jnp.concatenate([cross.T, last], axis=1)], axis=0)
    snap_gram = jnp.concatenate([snap_gram, jnp.zeros((new, half - new), jnp.float32)], axis=1)
    lane = lax.broadcasted_iota(jnp.int32, (modes, half), 1)
    line = lax.broadcasted_iota(jnp.int32, (modes, half), 0)
    wide = lax.broadcasted_iota(jnp.int32, (new, half), 1)
    unit = (wide == lax.broadcasted_iota(jnp.int32, (new, half), 0)).astype(jnp.float32)
    sigma = jnp.concatenate([jnp.zeros((1, count), jnp.float32), sigma_ref[...]], axis=1)
    early = jnp.concatenate([jnp.zeros((1, new), jnp.float32), sigma_ref[...], jnp.zeros((1, modes), jnp.float32)], axis=1)

    def at(place, x):
        above = [jnp.zeros((place, x.shape[1]), x.dtype)] if place else []
        under = half - place - x.shape[0]
        return jnp.concatenate(above + [x] + ([jnp.zeros((under, x.shape[1]), x.dtype)] if under else []), axis=0)

    corr = jnp.where(lane >= count, upper, 0.0)
    same = jnp.where(lane == count + line, 1.0, 0.0)
    twice = 2.0 * same - corr
    sent = jnp.concatenate([upper, lower, lower], axis=0)
    late = lax.broadcasted_iota(jnp.int32, (new, half), 0) >= modes + modes // 2
    sent = jnp.where((wide >= new) & ((wide >= count) == late), sent, 0.0)
    above = jnp.zeros((new, half), jnp.float32)
    joined_t = dot(sent, jnp.concatenate([above, twice, twice], axis=0))
    pick = jnp.concatenate([above, same, same], axis=0).astype(jnp.bfloat16)
    first_t = product_of(jnp.concatenate(pieces(sent), axis=1), jnp.concatenate([pick] * 3, axis=0))
    joined = dot(twice, at(0, first_t), NT)
    rest = first_t - dot(joined_t, at(count, corr))
    residual = (
        snap_gram - dot(joined_t, at(0, first_t), NT) - dot(rest, at(0, joined_t), NT)
    )
    corner = jnp.where(lane == count + line, sigma * sigma, 0.0) + dot(joined, at(count, joined), NT)
    scaling = jnp.where(lane == new + line, early * early, 0.0)
    bend = dot(joined, at(0, residual))

    step = jnp.concatenate(
        [
            at(0, unit + joined_t) + at(count, joined + scaling + corner),
            at(0, residual + joined_t) + at(count, bend + corner),
        ],
        axis=1,
    )
    step_ref[...] = as_right(step, 0)

    def iterate(_, parts):
        left, right = normalize(*parts, [parts[1]])
        after = product_of(as_left(right), step_ref[...])
        left, *after = normalize(left, right, [after[:, :half], after[:, half:]])
        frame_ref[...] = left
        return tuple(after)

    start = (joined + scaling + corner, bend + corner)
    after, _ = lax.fori_loop(0, ITERS, iterate, start)
    left = frame_ref[...]

    high, low_part = split(left[:, :count])
    left_side = jnp.concatenate(
        [jnp.concatenate([high, high], axis=1), jnp.concatenate([low_part, low_part], axis=1)], axis=0
    )
    for load in loads:
        load.wait()
    stores = []
    for i in range(columns // width):
        piece = pl.ds(i * width, width)
        data = jnp.concatenate(split(data_ref[:, piece]), axis=0)
        product = lax.dot_general(left_side, data, NN, preferred_element_type=jnp.float32)
        out_ref[:, piece] = product[:modes] + product[modes:]
        store = pltpu.make_async_copy(out_ref.at[:, piece], modes_ref.at[:, piece], out_sem.at[i])
        store.start()
        stores.append(store)

    part = jnp.where(lane < new, after, left * sigma)
    values_ref[...] = jnp.sqrt(dot(jnp.ones((8, half), jnp.float32), part * part, NT)[:1])
    for store in stores:
        store.wait()


def update(sums, sigma, snapshots, basis):
    new, columns = snapshots.shape
    modes = basis.shape[0]
    count = new + modes
    width = blocks_of(columns, 1024)
    half = count + modes
    return pl.pallas_call(
        functools.partial(update_kernel, width),
        out_shape=(
            jax.ShapeDtypeStruct((modes, columns), jnp.float32),
            jax.ShapeDtypeStruct((1, modes), jnp.float32),
        ),
        in_specs=[
            pl.BlockSpec(memory_space=pltpu.VMEM),
            pl.BlockSpec(memory_space=pltpu.VMEM),
            pl.BlockSpec(memory_space=pltpu.HBM),
            pl.BlockSpec(memory_space=pltpu.HBM),
        ],
        out_specs=(pl.BlockSpec(memory_space=pltpu.HBM), pl.BlockSpec(memory_space=pltpu.VMEM)),
        scratch_shapes=[
            pltpu.VMEM((count, columns), jnp.float32),
            pltpu.VMEM((modes, columns), jnp.float32),
            pltpu.VMEM((6 * half, 2 * half), jnp.bfloat16),
            pltpu.VMEM((modes, half), jnp.float32),
            pltpu.SemaphoreType.DMA((2,)),
            pltpu.SemaphoreType.DMA((columns // width,)),
        ],
        compiler_params=pltpu.CompilerParams(vmem_limit_bytes=GRANT),
        name="update",
    )(sums, sigma, snapshots, basis)


def per_device(sizes, basis, sigma, snapshots):
    total = basis.shape[1] * 1.0
    for _, size in sizes:
        total *= size
    basis = pltpu.with_memory_space_constraint(basis, pltpu.HBM)
    snapshots = pltpu.with_memory_space_constraint(snapshots, pltpu.HBM)
    sums = all_sum(gram(snapshots, basis, total), sizes)
    modes, values = update(sums, sigma.reshape(1, -1), snapshots, basis)
    return modes, values.reshape(-1)


def solution(mesh):
    placed = (P(None, AXES), P(), P(None, AXES))
    sizes = tuple((axis, mesh.shape[axis]) for axis in AXES)
    return jax.shard_map(
        functools.partial(per_device, sizes),
        mesh=mesh,
        in_specs=placed,
        out_specs=(P(None, AXES), P()),
        check_vma=False,
    )
```
